256 devices in a mesh: section: 8 (over z_hi, x), rep: 32 (over z_lo, y, core).
Axes of the slice: x: 4, y: 4, z: 8 (z_hi: 2, z_lo: 4; z = z_hi * 4 + z_lo), core: 2. Of those that a mesh axis runs over, the one named last changes fastest.
Arguments:
- layer_in: bfloat16 [8, 128, 4096], P('section', 'rep'), may hold values from -6 to 6
- next_in: bfloat16 [8, 128, 4096], P('section', 'rep'), may hold values from -6 to 6
- returned: bfloat16 [8, 256, 4096], P('section', 'rep'), may hold values from -6 to 6
- norm_gain: float32 [8, 4096], P('section'), may hold values from 0.25 to 1.75
- gate_weight: bfloat16 [8, 4096, 14336], P('section', None, 'rep'), may hold values from -0.09375 to 0.09375
- up_weight: bfloat16 [8, 4096, 14336], P('section', None, 'rep'), may hold values from -0.09375 to 0.09375
- down_weight: bfloat16 [8, 14336, 4096], P('section', 'rep'), may hold values from -0.046875 to 0.046875
- wiring: int32 [8, 32, 32], P('section'), may hold values from 0 to 2, as said below
Outputs:
- forwarded: bfloat16 [8, 256, 4096], P('section', 'rep')
- input_grad: bfloat16 [8, 128, 4096], P('section', 'rep')
- next_out: bfloat16 [8, 128, 4096], P('section', 'rep')
The draws below stay inside these ranges and needn't reach their ends.
Inputs may be any that keep to these rules, and one draw needn't show every extreme that they name: For every position p and row group r the entries wiring[p, r, :] sum to 2. For every position p and receiver j the column wiring[p, :, j] sums to at most 4, and in every position some column sums to exactly 4. In every position some row group sends all its 2 blocks to one receiver, and some receiver gets none.
All inputs are finite; a program needn't handle non-finite values.
Results may differ from the reference program's by a relative error of at most 0.035.
Values may be sent and summed in bfloat16 or wider, within the bound.
No kernel may reach another device: no remote copies, remote signals or barrier semaphores. Data moves between devices by JAX's collectives and lax.ppermute only.
A program may use at most 128 MiB of HBM per device.

```python
import jax
import jax.numpy as jnp
from jax import lax

D = 4096
FF = 14336
ROWS = 4
BLK = 2
POSITIONS = 8
NB = 2
CAP = 4
TOKENS = 128
SLOTS = 256
N_SECTION = 8
N_REP = 32


def draw_section(section_key):
    key_pair, key_shift, key_shuffle, key_row = jax.random.split(section_key, 4)
    half_count = N_REP // 2
    pairing = jax.random.permutation(key_pair, N_REP)
    load_shift = jax.random.randint(key_shift, (half_count,), 0, NB + 1).astype(jnp.int32)
    load_shift = load_shift.at[0].set(NB)
    receiver_loads = jnp.zeros((N_REP,), jnp.int32)
    receiver_loads = receiver_loads.at[pairing[:half_count]].set(NB + load_shift)
    receiver_loads = receiver_loads.at[pairing[half_count:]].set(NB - load_shift)
    rest_loads = receiver_loads.at[pairing[0]].add(-NB)
    rest_dest = jnp.repeat(jnp.arange(N_REP, dtype=jnp.int32), rest_loads, total_repeat_length=(N_REP - 1) * NB)
    rest_dest = jax.random.permutation(key_shuffle, rest_dest)
    full_row = jnp.full((NB,), pairing[0], jnp.int32)
    destinations = jnp.concatenate([full_row, rest_dest]).astype(jnp.int32)
    per_sender = destinations.reshape(N_REP, NB)
    row_shift = jax.random.randint(key_row, (), 0, N_REP).astype(jnp.int32)
    per_sender = jnp.roll(per_sender, row_shift, axis=0)
    member_ids = jnp.arange(N_REP, dtype=jnp.int32)
    return jnp.sum((per_sender[:, :, None] == member_ids[None, None, :]).astype(jnp.int32), axis=1).astype(jnp.int32)


def draw_wiring(key, part):
    section_keys = jax.random.split(key, N_SECTION)
    return jax.vmap(draw_section)(section_keys)


def block_levels(rng, dims, shards, least, top_value):
    loudness, own = 1.0, jax.random.fold_in(rng, 6)
    for position, shards_of in shards:
        draws = jnp.exp(jax.random.uniform(jax.random.fold_in(own, position), (shards_of,), jnp.float32, least / len(shards), top_value / len(shards)))
        loudness = loudness * jnp.repeat(draws, dims[position] // shards_of).reshape([-1 if axis == position else 1 for axis in range(len(dims))])
    return loudness


def gaussian(rng, shape, deviation, bound, cuts=(), kind=jnp.bfloat16):
    drawn = deviation * jax.random.normal(rng, shape, jnp.float32)
    if cuts:
        drawn = drawn * block_levels(rng, shape, cuts, -0.22, 0.18)
    return jnp.clip(drawn, -bound, bound).astype(kind)


def setup_inputs(seed: int = 0) -> dict:
    splits = jax.random.split(jax.random.key(seed), 9)
    return {
        "layer_in": gaussian(splits[0], (POSITIONS, TOKENS, D), 1.0, 6.0, ((0, 8), (1, 32))),
        "next_in": gaussian(splits[1], (POSITIONS, TOKENS, D), 1.0, 6.0, ((0, 8), (1, 32))),
        "returned": gaussian(splits[2], (POSITIONS, SLOTS, D), 1.0, 6.0, ((0, 8), (1, 32))),
        "norm_gain": jnp.clip(1.0 + 0.15 * jax.random.normal(splits[3], (POSITIONS, D), jnp.float32), 0.25, 1.75),
        "gate_weight": gaussian(splits[4], (POSITIONS, D, FF), D ** -0.5, 0.09375, ((0, 8), (2, 32))),
        "up_weight": gaussian(splits[5], (POSITIONS, D, FF), D ** -0.5, 0.09375, ((0, 8), (2, 32))),
        "down_weight": gaussian(splits[6], (POSITIONS, FF, D), FF ** -0.5, 0.046875, ((0, 8), (1, 32))),
        "wiring": draw_wiring(jax.random.fold_in(splits[8], 71), 0),
    }


epsilon = 1e-05
step_rate = 0.5

def route_tables(wiring_section, replicas, blocks_dev, capacity):
    counts = wiring_section.astype(jnp.int32)
    row_total = jnp.cumsum(counts, axis=1).astype(jnp.int32)
    column_total = jnp.cumsum(counts, axis=0).astype(jnp.int32)
    row_start = (row_total - counts).astype(jnp.int32)
    column_start = (column_total - counts).astype(jnp.int32)
    slot_ids = jnp.arange(capacity, dtype=jnp.int32)
    block_ids = jnp.arange(blocks_dev, dtype=jnp.int32)
    member_ids = jnp.arange(replicas, dtype=jnp.int32)
    sender = lax.optimization_barrier(jnp.sum((column_total.T[:, :, None] <= slot_ids[None, None, :]).astype(jnp.int32), axis=1)).astype(jnp.int32)
    slot_live = slot_ids[None, :] < column_total[replicas - 1][:, None]
    sender = jnp.minimum(sender, replicas - 1)
    within = slot_ids[None, :] - column_start[sender, member_ids[:, None]]
    within = jnp.where(slot_live, within, 0).astype(jnp.int32)
    local_source = (sender * blocks_dev + within).astype(jnp.int32)
    global_source = (sender * blocks_dev + row_start[sender, member_ids[:, None]] + within).astype(jnp.int32)
    target_member = lax.optimization_barrier(jnp.sum((row_total[:, None, :] <= block_ids[None, :, None]).astype(jnp.int32), axis=2)).astype(jnp.int32)
    target_member = jnp.minimum(target_member, replicas - 1)
    block_offset = (block_ids[None, :] - row_start[member_ids[:, None], target_member]).astype(jnp.int32)
    global_target = (target_member * capacity + column_start[member_ids[:, None], target_member] + block_offset).astype(jnp.int32)
    local_target = (target_member * blocks_dev + block_offset).astype(jnp.int32)
    return (counts, row_start, column_start, slot_live, local_source, global_source, global_target, local_target)

def down_product(operands):
    return jnp.dot(operands[0], operands[1], preferred_element_type=jnp.float32)

def normalize(layer_rows, gain_row):
    values = layer_rows.astype(jnp.float32)
    row_scale = lax.rsqrt(lax.optimization_barrier(jnp.mean(values * values, axis=1, keepdims=True)) + epsilon)
    normed = (values * row_scale * gain_row[None, :]).astype(jnp.bfloat16)
    return (values, row_scale, normed)

def down_sum(hidden, down_weight, values):
    shard_units = FF // N_REP
    hidden_parts = hidden.reshape(TOKENS, N_REP, shard_units).transpose(1, 0, 2)
    down_parts = down_weight.reshape(N_REP, shard_units, D)
    partial_value = lax.map(down_product, (hidden_parts, down_parts))
    owner_term = jnp.eye(N_REP, dtype=jnp.float32)[:, :, None, None] * values.reshape(1, N_REP, ROWS, D)
    shard_terms = (partial_value.reshape(N_REP, N_REP, ROWS, D) + owner_term).astype(jnp.bfloat16)
    shard_terms = lax.optimization_barrier(shard_terms)
    return lax.optimization_barrier(jnp.sum(shard_terms.astype(jnp.float32), axis=0)).reshape(TOKENS, D).astype(jnp.bfloat16)

def section_forward(layer_rows, gain_row, gate_weight, up_weight, down_weight):
    values, row_scale, normed = normalize(layer_rows, gain_row)
    gate_act = jnp.dot(normed, gate_weight, preferred_element_type=jnp.float32)
    up_act = jnp.dot(normed, up_weight, preferred_element_type=jnp.float32)
    hidden = (jax.nn.silu(gate_act) * up_act).astype(jnp.bfloat16)
    layer_out = down_sum(hidden, down_weight, values)
    return (layer_out, values, row_scale, normed, gate_act, up_act, hidden)

def next_forward(layer_rows, gain_row, own_gate, mate_gate, own_up, mate_up, averaged_down):
    values, row_scale, normed = normalize(layer_rows, gain_row)
    gate_act = 0.5 * (jnp.dot(normed, own_gate, preferred_element_type=jnp.float32) + jnp.dot(normed, mate_gate, preferred_element_type=jnp.float32))
    up_act = 0.5 * (jnp.dot(normed, own_up, preferred_element_type=jnp.float32) + jnp.dot(normed, mate_up, preferred_element_type=jnp.float32))
    hidden = (jax.nn.silu(gate_act) * up_act).astype(jnp.bfloat16)
    return down_sum(hidden, averaged_down, values)

def backward_term(operands):
    dgate_part, dup_part, gate_part, up_part = operands
    contract = (((1,), (1,)), ((), ()))
    first = lax.dot_general(dgate_part, gate_part, contract, preferred_element_type=jnp.float32)
    second = lax.dot_general(dup_part, up_part, contract, preferred_element_type=jnp.float32)
    return (first + second).astype(jnp.bfloat16)

def section_backward(cotangent, values, row_scale, gain_row, normed, gate_act, up_act, hidden, gate_weight, up_weight, down_weight):
    dhidden = jnp.dot(cotangent, down_weight.T, preferred_element_type=jnp.float32)
    sigmoid_gate = jax.nn.sigmoid(gate_act)
    silu_gate = gate_act * sigmoid_gate
    grad_gate_act = (dhidden * up_act * sigmoid_gate * (1.0 + gate_act * (1.0 - sigmoid_gate))).astype(jnp.bfloat16)
    grad_up_act = (dhidden * silu_gate).astype(jnp.bfloat16)
    shard_units = FF // N_REP
    gate_parts = gate_weight.reshape(D, N_REP, shard_units).transpose(1, 0, 2)
    up_parts = up_weight.reshape(D, N_REP, shard_units).transpose(1, 0, 2)
    dgate_parts = grad_gate_act.reshape(TOKENS, N_REP, shard_units).transpose(1, 0, 2)
    dup_parts = grad_up_act.reshape(TOKENS, N_REP, shard_units).transpose(1, 0, 2)
    dterms = lax.map(backward_term, (dgate_parts, dup_parts, gate_parts, up_parts))
    dterms = lax.optimization_barrier(dterms)
    dnormed = lax.optimization_barrier(jnp.sum(dterms.astype(jnp.float32), axis=0))
    scaled_grad = gain_row[None, :] * dnormed
    input_grad = (cotangent.astype(jnp.float32) + row_scale * scaled_grad - values * row_scale ** 3 * lax.optimization_barrier(jnp.mean(values * scaled_grad, axis=1, keepdims=True))).astype(jnp.bfloat16)
    grad_gate = jnp.dot(normed.T, grad_gate_act, preferred_element_type=jnp.float32)
    grad_up = jnp.dot(normed.T, grad_up_act, preferred_element_type=jnp.float32)
    grad_down = jnp.dot(hidden.T, cotangent, preferred_element_type=jnp.float32)
    return (input_grad, grad_gate, grad_up, grad_down)

def apply_update(weight, gradient):
    updated = (weight.astype(jnp.float32) - step_rate / TOKENS * gradient).astype(jnp.bfloat16)
    return lax.optimization_barrier(updated)

def reference(layer_in, next_in, returned, norm_gain, gate_weight, up_weight, down_weight, wiring):
    forwarded_list = [None] * N_SECTION
    input_grads = [None] * N_SECTION
    next_outs = [None] * N_SECTION
    half_count = N_SECTION // 2
    for section_index in range(half_count):
        members = (section_index, section_index + half_count)
        updated_sets = {}
        for place in members:
            following = (place + 1) % N_SECTION
            layer_out, values, row_scale, normed, gate_act, up_act, hidden = section_forward(layer_in[place], norm_gain[place], gate_weight[place], up_weight[place], down_weight[place])
            tables = route_tables(wiring[place], N_REP, NB, CAP)
            slot_live, global_source, global_target = (tables[3], tables[5], tables[6])
            out_blocks = layer_out.reshape(N_REP * NB, BLK, D)
            slot_blocks = jnp.take(out_blocks, global_source.reshape(-1), axis=0).reshape(N_REP, CAP, BLK, D)
            slot_blocks = jnp.where(slot_live[:, :, None, None], slot_blocks, jnp.zeros((), jnp.bfloat16))
            forwarded_list[following] = slot_blocks.reshape(SLOTS, D)
            later_slots = returned[following].reshape(N_REP * CAP, BLK, D)
            cotangent = jnp.take(later_slots, global_target.reshape(-1), axis=0).reshape(TOKENS, D)
            input_grad, grad_gate, grad_up, grad_down = section_backward(cotangent, values, row_scale, norm_gain[place], normed, gate_act, up_act, hidden, gate_weight[place], up_weight[place], down_weight[place])
            input_grads[place] = input_grad
            updated_sets[place] = (apply_update(gate_weight[place], grad_gate), apply_update(up_weight[place], grad_up), apply_update(down_weight[place], grad_down))
        for place in members:
            partner = (place + half_count) % N_SECTION
            own_set = updated_sets[place]
            mate_set = updated_sets[partner]
            averaged_down = ((own_set[2].astype(jnp.float32) + mate_set[2].astype(jnp.float32)) * 0.5).astype(jnp.bfloat16)
            next_outs[place] = next_forward(next_in[place], norm_gain[place], own_set[0], mate_set[0], own_set[1], mate_set[1], averaged_down)
    return (jnp.stack(forwarded_list), jnp.stack(input_grads), jnp.stack(next_outs))
```

```python
import jax
import jax.numpy as jnp
from jax import lax
from jax.sharding import PartitionSpec as P

BLK = 2
NZ = 4
NY = 4
NC = 2

epsilon = 1e-05
step_rate = 0.5

F32 = jnp.float32
BF16 = jnp.bfloat16


def send(value, ds=0, dz=0, dy=0, dc=0):
    sections = lax.axis_size("section")
    replicas = lax.axis_size("rep")
    pairs = []
    for s in range(sections):
        for z in range(NZ):
            for y in range(NY):
                for c in range(NC):
                    source = s * replicas + (z * NY + y) * NC + c
                    target = (
                        ((s + ds) % sections) * replicas
                        + (((z + dz) % NZ) * NY + (y + dy) % NY) * NC
                        + (c + dc) % NC
                    )
                    pairs.append((source, target))
    return lax.ppermute(value, ("section", "rep"), pairs)


def group_at(index):
    me = lax.axis_index("rep")
    z, y, c = me // (NY * NC), (me // NC) % NY, me % NC
    dz, dy, dc = index % NZ, (index // NZ) % NY, index // (NZ * NY)
    return (((z + dz) % NZ) * NY + (y + dy) % NY) * NC + (c + dc) % NC


def routing(wiring, blocks_dev, capacity):
    groups = wiring.shape[0]
    rows = groups * blocks_dev * BLK
    slots = groups * capacity * BLK
    counts = wiring.astype(BF16)
    row_id = lax.broadcasted_iota(jnp.int32, (rows, groups), 0)
    row_member = lax.broadcasted_iota(jnp.int32, (rows, groups), 1)
    row_group = group_at(row_id // (blocks_dev * BLK))
    left = jnp.concatenate(
        [(row_member == row_group).astype(BF16), (row_member < row_group).astype(BF16)], axis=0
    )
    slot_id = lax.broadcasted_iota(jnp.int32, (groups, slots), 1)
    slot_member = lax.broadcasted_iota(jnp.int32, (groups, slots), 0)
    slot_group = group_at(slot_id // (capacity * BLK))
    right = jnp.concatenate(
        [(slot_member == slot_group).astype(BF16), (slot_member < slot_group).astype(BF16)], axis=1
    )
    half = jnp.dot(left, counts, preferred_element_type=F32).astype(BF16)
    table = jnp.dot(half, right, preferred_element_type=F32).astype(jnp.int32)
    count = table[:rows, :slots]
    row_start = table[:rows, slots:]
    column_start = table[rows:, :slots]
    r = lax.broadcasted_iota(jnp.int32, (rows, slots), 0)
    q = lax.broadcasted_iota(jnp.int32, (rows, slots), 1)
    block = (r % (blocks_dev * BLK)) // BLK
    place = (q % (capacity * BLK)) // BLK
    offset = block - row_start
    hit = (offset >= 0) & (offset < count) & (place == column_start + offset)
    return (hit & (r % BLK == q % BLK)).astype(BF16)


def normalize(layer_rows, gain_row):
    values = layer_rows.astype(F32)
    row_scale = lax.rsqrt(jnp.mean(values * values, axis=1, keepdims=True) + epsilon)
    return values, row_scale, (values * row_scale * gain_row[None, :]).astype(BF16)


def dot(a, b, ca=1, cb=0):
    return lax.dot_general(a, b, (((ca,), (cb,)), ((), ())), preferred_element_type=F32)


def add_up(parts):
    total = parts[0].astype(F32)
    for part in parts[1:]:
        total = total + part.astype(F32)
    return total


def cut(value, count):
    size = value.shape[0] // count
    return [value[i * size : (i + 1) * size] for i in range(count)]


def per_device(layer_in, next_in, returned, norm_gain, gate_weight, up_weight, down_weight, wiring):
    half_ring = lax.axis_size("section") // 2
    first_half = lax.axis_index("section") < half_ring
    row_count = layer_in.shape[1]
    blocks_dev = row_count // BLK
    capacity = returned.shape[1] // BLK
    token_count = row_count * lax.axis_size("rep")
    gain_row = norm_gain[0]
    gate_local, up_local, down_local = gate_weight[0], up_weight[0], down_weight[0]
    slot_rows = returned[0]

    values, row_scale, normed = normalize(layer_in[0], gain_row)
    next_values, _, next_normed = normalize(next_in[0], gain_row)
    route = routing(wiring[0], blocks_dev, capacity)

    slots_z = [send(slot_rows, ds=-1, dz=-k) for k in range(NZ)]
    normed_z = [normed] + [send(normed, dz=-k) for k in range(1, NZ)]
    own_z = [next_normed] + [send(next_normed, dz=-k) for k in range(1, NZ)]
    mate_z = [send(next_normed, ds=half_ring, dz=-k) for k in range(NZ)]
    block_a = jnp.concatenate(slots_z + normed_z, axis=0)
    own_z, mate_z = jnp.concatenate(own_z, axis=0), jnp.concatenate(mate_z, axis=0)
    block_n = jnp.concatenate(
        [jnp.where(first_half, own_z, mate_z), jnp.where(first_half, mate_z, own_z)], axis=0
    )
    a_y = [block_a] + [send(block_a, dy=-k) for k in range(1, NY)]
    a_all = a_y + [send(a, dc=1) for a in a_y]
    n_y = [block_n] + [send(block_n, dy=-k) for k in range(1, NY)]
    n_all = n_y + [send(n, dc=1) for n in n_y]
    cut_at = NZ * slot_rows.shape[0]
    slots_all = jnp.concatenate([a[:cut_at] for a in a_all], axis=0)
    normed_all = jnp.concatenate([a[cut_at:] for a in a_all], axis=0)
    next_all = jnp.concatenate(n_all, axis=0)

    gate_act = dot(normed_all, gate_local)
    up_act = dot(normed_all, up_local)
    sigmoid_gate = jax.nn.sigmoid(gate_act)
    silu_gate = gate_act * sigmoid_gate
    hidden = (silu_gate * up_act).astype(BF16)
    term = dot(hidden, down_local)
    term = jnp.concatenate([term[:row_count] + values, term[row_count:]], axis=0).astype(BF16)
    term_slots = dot(route, term, 0, 0).astype(BF16)

    cotangent = dot(route, slots_all).astype(BF16)
    dhidden = dot(cotangent, down_local, 1, 1)
    grad_gate_act = (
        dhidden * up_act * sigmoid_gate * (1.0 + gate_act * (1.0 - sigmoid_gate))
    ).astype(BF16)
    grad_up_act = (dhidden * silu_gate).astype(BF16)
    dterm = (
        dot(grad_gate_act, gate_local, 1, 1) + dot(grad_up_act, up_local, 1, 1)
    ).astype(BF16)

    update_factor = step_rate / token_count
    updated_gate = (
        gate_local.astype(F32) - update_factor * dot(normed_all, grad_gate_act, 0, 0)
    ).astype(BF16)
    updated_up = (
        up_local.astype(F32) - update_factor * dot(normed_all, grad_up_act, 0, 0)
    ).astype(BF16)
    updated_down = (
        down_local.astype(F32) - update_factor * dot(hidden, cotangent, 0, 0)
    ).astype(BF16)
    gate_part = dot(next_all, updated_gate)
    mate_gate = send(gate_part.astype(BF16), ds=half_ring)
    up_part = dot(next_all, updated_up)
    mate_up = send(up_part.astype(BF16), ds=half_ring)
    gate_next = 0.5 * (gate_part + mate_gate.astype(F32))
    up_next = 0.5 * (up_part + mate_up.astype(F32))
    hidden_next = (jax.nn.silu(gate_next) * up_next).astype(BF16)
    term_next = (0.5 * dot(hidden_next, updated_down)).astype(BF16)

    def core_sum(terms):
        mine, other = cut(terms, NC)
        return add_up([mine, send(other, dc=1)]).astype(BF16)

    def y_sum(terms):
        parts = cut(terms, NY)
        return add_up(
            [parts[0]] + [send(parts[k], dy=k) for k in range(1, NY)]
        ).astype(BF16)

    slot_sum = y_sum(core_sum(term_slots))
    slot_parts = cut(slot_sum, NZ)
    forwarded = add_up([send(slot_parts[k], ds=1, dz=k) for k in range(NZ)]).astype(BF16)

    dparts = cut(y_sum(core_sum(dterm)), NZ)
    dnormed = add_up([dparts[0]] + [send(dparts[k], dz=k) for k in range(1, NZ)])
    scaled_grad = gain_row[None, :] * dnormed
    input_grad = (
        cotangent[:row_count].astype(F32)
        + row_scale * scaled_grad
        - values * row_scale**3 * jnp.mean(values * scaled_grad, axis=1, keepdims=True)
    ).astype(BF16)

    first, second = cut(y_sum(core_sum(term_next)), 2)
    own_part = jnp.where(first_half, first, second)
    mate_part = jnp.where(first_half, second, first)
    pair_sum = add_up([own_part, send(mate_part, ds=half_ring)]).astype(BF16)
    nparts = cut(pair_sum, NZ)
    next_out = add_up(
        [next_values, nparts[0]] + [send(nparts[k], dz=k) for k in range(1, NZ)]
    ).astype(BF16)
    return (forwarded[None], input_grad[None], next_out[None])


def solution(mesh):
    in_specs = (
        P("section", "rep", None),
        P("section", "rep", None),
        P("section", "rep", None),
        P("section", None),
        P("section", None, "rep"),
        P("section", None, "rep"),
        P("section", "rep", None),
        P("section", None, None),
    )
    out_specs = (P("section", "rep", None), P("section", "rep", None), P("section", "rep", None))
    return jax.shard_map(
        per_device, mesh=mesh, in_specs=in_specs, out_specs=out_specs, check_vma=False
    )
```

```python
import functools

import jax
import jax.numpy as jnp
from jax import lax
from jax.experimental import pallas as pl
from jax.experimental.pallas import tpu as pltpu
from jax.sharding import PartitionSpec as P

BLK = 2
NZ = 4
NY = 4
NC = 2

epsilon = 1e-05
step_rate = 0.5

F32 = jnp.float32
BF16 = jnp.bfloat16
WIDTH = 1024
VMEM_LIMIT = 18 << 20


def send(value, ds=0, dz=0, dy=0, dc=0):
    sections = lax.axis_size("section")
    replicas = lax.axis_size("rep")
    pairs = []
    for s in range(sections):
        for z in range(NZ):
            for y in range(NY):
                for c in range(NC):
                    source = s * replicas + (z * NY + y) * NC + c
                    target = (
                        ((s + ds) % sections) * replicas
                        + (((z + dz) % NZ) * NY + (y + dy) % NY) * NC
                        + (c + dc) % NC
                    )
                    pairs.append((source, target))
    return lax.ppermute(value, ("section", "rep"), pairs)


def group_at(index):
    me = lax.axis_index("rep")
    z, y, c = me // (NY * NC), (me // NC) % NY, me % NC
    dz, dy, dc = index % NZ, (index // NZ) % NY, index // (NZ * NY)
    return (((z + dz) % NZ) * NY + (y + dy) % NY) * NC + (c + dc) % NC


def selection(wiring, blocks_dev, capacity):
    groups = wiring.shape[0]
    per_group = blocks_dev * BLK
    per_slots = capacity * BLK
    per_unit = per_slots + per_group
    rows, columns = groups * per_group, groups * per_unit
    counts = wiring.astype(BF16)
    row_id = lax.broadcasted_iota(jnp.int32, (rows, groups), 0)
    row_member = lax.broadcasted_iota(jnp.int32, (rows, groups), 1)
    row_group = group_at(row_id // per_group)
    left = jnp.concatenate(
        [(row_member == row_group).astype(BF16), (row_member < row_group).astype(BF16)], axis=0
    )
    column_id = lax.broadcasted_iota(jnp.int32, (groups, columns), 1)
    column_member = lax.broadcasted_iota(jnp.int32, (groups, columns), 0)
    column_group = group_at(column_id // per_unit)
    right = jnp.concatenate(
        [(column_member == column_group).astype(BF16), (column_member < column_group).astype(BF16)],
        axis=1,
    )
    half = jnp.dot(left, counts, preferred_element_type=F32).astype(BF16)
    table = jnp.dot(half, right, preferred_element_type=F32).astype(jnp.int32)
    count = table[:rows, :columns]
    row_start = table[:rows, columns:]
    column_start = table[rows:, :columns]
    r = lax.broadcasted_iota(jnp.int32, (rows, columns), 0)
    q = lax.broadcasted_iota(jnp.int32, (rows, columns), 1)
    inner = q % per_unit
    block = (r % per_group) // BLK
    offset = block - row_start
    hit = (offset >= 0) & (offset < count) & (inner // BLK == column_start + offset)
    hit = hit & (inner < per_slots) & (r % BLK == inner % BLK)
    plain = (q // per_unit == r // per_group) & (inner == per_slots + r % per_group)
    chosen = jnp.concatenate([hit.astype(BF16), plain.astype(BF16)], axis=0)
    return lax.optimization_barrier(chosen)


def normalize(layer_rows, gain_row):
    values = layer_rows.astype(F32)
    row_scale = lax.rsqrt(jnp.mean(values * values, axis=1, keepdims=True) + epsilon)
    return values, row_scale, (values * row_scale * gain_row[None, :]).astype(BF16)


def dot(a, b, ca=1, cb=0):
    return lax.dot_general(a, b, (((ca,), (cb,)), ((), ())), preferred_element_type=F32)


def after(value, *others):
    return lax.optimization_barrier((value, *others))[0]


def add_up(parts):
    total = parts[0].astype(F32)
    for part in parts[1:]:
        total = total + part.astype(F32)
    return total


def cut(value, count):
    size = value.shape[0] // count
    return [value[i * size : (i + 1) * size] for i in range(count)]


def core_sum(terms):
    mine, other = cut(terms, NC)
    return add_up([mine, send(other, dc=1)]).astype(BF16)


def y_sum(terms):
    parts = cut(terms, NY)
    return add_up(
        [parts[0]] + [send(parts[k], dy=k) for k in range(1, NY)]
    ).astype(BF16)


def dot_t(a, b):
    return dot(a, b, 1, 1)


def first_kernel(count, factor, *refs):
    select = refs[0]
    blocks, nexts = refs[1 : 1 + count], refs[1 + count : 1 + 2 * count]
    gate_w, up_w, down_w = refs[1 + 2 * count : 4 + 2 * count]
    cot_out, hidden_out, dgate_out, dup_out, gate_out, up_out, gate_sent, up_sent = refs[
        4 + 2 * count : 12 + 2 * count
    ]
    gate_sum, up_sum, dhidden_sum, inner_sum = refs[12 + 2 * count :]
    step = pl.program_id(0)
    tokens = dhidden_sum.shape[0]
    chosen = dot(select[...], jnp.concatenate([r[...] for r in blocks], axis=0)).astype(BF16)
    cotangent, normed = chosen[:tokens], chosen[tokens:]
    cot_out[...] = cotangent
    ahead = jnp.concatenate([r[...] for r in nexts], axis=0)
    rows = jnp.concatenate([normed, ahead], axis=0)
    gate = dot_t(rows, gate_w[...])
    up = dot_t(rows, up_w[...])
    dhidden = dot_t(cotangent, down_w[...])
    inner = dot_t(ahead, normed)

    @pl.when(step == 0)
    def _():
        gate_sum[...] = gate
        up_sum[...] = up
        dhidden_sum[...] = dhidden
        inner_sum[...] = inner

    @pl.when(step > 0)
    def _():
        gate_sum[...] += gate
        up_sum[...] += up
        dhidden_sum[...] += dhidden
        inner_sum[...] += inner

    @pl.when(step == pl.num_programs(0) - 1)
    def _():
        gate_act, up_act = gate_sum[:tokens], up_sum[:tokens]
        sigmoid_gate = jax.nn.sigmoid(gate_act)
        silu_gate = gate_act * sigmoid_gate
        grad = dhidden_sum[...]
        hidden_out[...] = (silu_gate * up_act).astype(BF16)
        dgate = (
            grad * up_act * sigmoid_gate * (1.0 + gate_act * (1.0 - sigmoid_gate))
        ).astype(BF16)
        dup = (grad * silu_gate).astype(BF16)
        dgate_out[...] = dgate
        dup_out[...] = dup
        overlap = (-factor * inner_sum[...]).astype(BF16)
        gate_next = gate_sum[tokens:] + dot(overlap, dgate)
        up_next = up_sum[tokens:] + dot(overlap, dup)
        gate_out[...] = gate_next
        up_out[...] = up_next
        gate_sent[...] = gate_next.astype(BF16)
        up_sent[...] = up_next.astype(BF16)


def second_kernel(
    spread, hidden, dgate, dup, own_rows, gate_w, up_w, down_w, out
):
    top = own_rows.shape[0]
    term = dot(hidden[...], down_w[...])
    term = jnp.concatenate([term[:top] + own_rows[...], term[top:]], axis=0)
    dterm = dot(dgate[...], gate_w[...]) + dot(dup[...], up_w[...])
    both = jnp.concatenate([term.astype(BF16), dterm.astype(BF16)], axis=0)
    out[...] = dot(spread[...], both).astype(BF16)


def third_kernel(
    factor, row_count, gate, up, mate_gate, mate_up, hidden, cotangent, down_w, out, hidden_next, overlap
):
    @pl.when(pl.program_id(0) == 0)
    def _():
        gate_next = 0.5 * (gate[...] + mate_gate[...].astype(F32))
        up_next = 0.5 * (up[...] + mate_up[...].astype(F32))
        units = (gate_next * jax.nn.sigmoid(gate_next) * up_next).astype(BF16)
        rows = units.shape[0]
        to = lax.broadcasted_iota(jnp.int32, (rows, rows), 0)
        at = lax.broadcasted_iota(jnp.int32, (rows, rows), 1)
        i, j = to & (row_count - 1), to // row_count
        z, replica, y, core = j & (NZ - 1), (j // NZ) & 1, (j // (2 * NZ)) & (NY - 1), j // (2 * NZ * NY)
        source = (((core * NZ + z) * NY + y) * 2 + replica) * row_count + i
        order = jnp.where(at == source, 1.0, 0.0).astype(BF16)
        units = dot(order, units).astype(BF16)
        hidden_next[...] = units
        overlap[...] = (-factor * dot_t(units, hidden[...])).astype(BF16)

    term = dot(hidden_next[...], down_w[...]) + dot(overlap[...], cotangent[...])
    out[...] = (0.5 * term).astype(BF16)


def whole(shape):
    return pl.BlockSpec(shape, lambda i: (0,) * len(shape))


def columns(rows, width):
    return pl.BlockSpec((rows, width), lambda i: (0, i))


def run(kernel, steps, in_specs, outs, out_specs, scratch, flops, name, args):
    moved = sum(a.size * a.dtype.itemsize for a in args)
    return pl.pallas_call(
        kernel,
        grid=(steps,),
        in_specs=in_specs,
        out_shape=outs,
        out_specs=out_specs,
        scratch_shapes=scratch,
        cost_estimate=pl.CostEstimate(flops=flops, bytes_accessed=moved, transcendentals=0),
        compiler_params=pltpu.CompilerParams(vmem_limit_bytes=VMEM_LIMIT),
        name=name,
    )(*args)


def per_device(layer_in, next_in, returned, norm_gain, gate_weight, up_weight, down_weight, wiring):
    half_ring = lax.axis_size("section") // 2
    first_half = lax.axis_index("section") < half_ring
    row_count = layer_in.shape[1]
    blocks_dev = row_count // BLK
    capacity = returned.shape[1] // BLK
    token_count = row_count * lax.axis_size("rep")
    gain_row = norm_gain[0]
    gate_local, up_local, down_local = gate_weight[0].T, up_weight[0].T, down_weight[0]
    slot_rows = returned[0]

    update_factor = step_rate / token_count
    width = layer_in.shape[2]
    units = gate_local.shape[0]
    chunk = min(WIDTH, width)
    steps = width // chunk

    shifted = send(slot_rows, ds=-1)
    next_values, _, next_normed = normalize(next_in[0], gain_row)
    mate_normed = send(next_normed, ds=half_ring)
    values, row_scale, normed = normalize(layer_in[0], gain_row)
    select = selection(wiring[0], blocks_dev, capacity)
    spread = lax.optimization_barrier(select.T)

    block_z = jnp.concatenate([shifted, normed], axis=0)
    block_y = jnp.concatenate(
        [block_z] + [send(block_z, dz=-k) for k in range(1, NZ)], axis=0
    )
    blocks = [block_y] + [send(block_y, dy=-k) for k in range(1, NY)]
    blocks = blocks + [send(block, dc=1) for block in blocks]
    next_y = jnp.concatenate(
        [
            jnp.where(first_half, next_normed, mate_normed),
            jnp.where(first_half, mate_normed, next_normed),
        ],
        axis=0,
    )
    next_z = jnp.concatenate([next_y] + [send(next_y, dy=-k) for k in range(1, NY)], axis=0)
    nexts = [next_z] + [send(next_z, dz=-k) for k in range(1, NZ)]
    nexts = nexts + [send(block, dc=1) for block in nexts]

    pair_tokens = 2 * token_count
    part = jax.ShapeDtypeStruct((token_count, units), BF16)
    product = jax.ShapeDtypeStruct((pair_tokens, units), F32)
    product_sent = jax.ShapeDtypeStruct((pair_tokens, units), BF16)
    per_row = 2 * width * units
    cotangent, hidden, grad_gate_act, grad_up_act, gate_part, up_part, gate_sent, up_sent = run(
        functools.partial(first_kernel, len(blocks), update_factor),
        steps,
        [whole(select.shape)]
        + [columns(block.shape[0], chunk) for block in blocks + nexts]
        + [columns(units, chunk)] * 3,
        [jax.ShapeDtypeStruct((token_count, width), BF16), part, part, part]
        + [product, product, product_sent, product_sent],
        [columns(token_count, chunk)]
        + [whole(part.shape)] * 3
        + [whole(product.shape)] * 4,
        [
            pltpu.VMEM((token_count + pair_tokens, units), F32),
            pltpu.VMEM((token_count + pair_tokens, units), F32),
            pltpu.VMEM((token_count, units), F32),
            pltpu.VMEM((pair_tokens, token_count), F32),
        ],
        per_row * token_count * 9,
        "first",
        [select] + blocks + nexts + [gate_local, up_local, down_local],
    )
    mate_gate = send(gate_sent, ds=half_ring)
    mate_up = send(up_sent, ds=half_ring)

    own_rows = jnp.concatenate([values, jnp.zeros_like(values)], axis=0)
    terms = run(
        second_kernel,
        steps,
        [whole(spread.shape)]
        + [whole(part.shape)] * 3
        + [columns(own_rows.shape[0], chunk)]
        + [columns(units, chunk)] * 3,
        jax.ShapeDtypeStruct((spread.shape[0], width), BF16),
        columns(spread.shape[0], chunk),
        [],
        per_row * token_count * 5,
        "second",
        [spread, hidden, grad_gate_act, grad_up_act, own_rows, gate_local, up_local, down_local],
    )
    both = y_sum(core_sum(terms))
    gate_part, up_part, both = lax.optimization_barrier((gate_part, up_part, both))

    term_next = run(
        functools.partial(third_kernel, update_factor, row_count),
        steps,
        [whole(product.shape)] * 4
        + [whole(part.shape), columns(token_count, chunk), columns(units, chunk)],
        jax.ShapeDtypeStruct((pair_tokens, width), BF16),
        columns(pair_tokens, chunk),
        [pltpu.VMEM((pair_tokens, units), BF16), pltpu.VMEM((pair_tokens, token_count), BF16)],
        per_row * token_count * 3,
        "third",
        [gate_part, up_part, mate_gate, mate_up, hidden, cotangent, down_local],
    )
    pair = core_sum(term_next)
    both = cut(after(both, pair), NZ)
    both = add_up([both[0]] + [send(both[k], dz=k) for k in range(1, NZ)])
    forwarded = send(both[: slot_rows.shape[0]].astype(BF16), ds=1)
    dnormed = both[slot_rows.shape[0] :]
    first, second = cut(after(y_sum(pair), both), 2)
    own_part = jnp.where(first_half, first, second)
    mate_part = jnp.where(first_half, second, first)
    pair_sum = add_up([own_part, send(mate_part, ds=half_ring)]).astype(BF16)
    nparts = cut(pair_sum, NZ)
    next_out = add_up(
        [next_values, nparts[0]] + [send(nparts[k], dz=k) for k in range(1, NZ)]
    ).astype(BF16)
    scaled_grad = gain_row[None, :] * dnormed
    input_grad = (
        cotangent[:row_count].astype(F32)
        + row_scale * scaled_grad
        - values * row_scale**3 * jnp.mean(values * scaled_grad, axis=1, keepdims=True)
    ).astype(BF16)
    return (forwarded[None], input_grad[None], next_out[None])


def solution(mesh):
    in_specs = (
        P("section", "rep", None),
        P("section", "rep", None),
        P("section", "rep", None),
        P("section", None),
        P("section", None, "rep"),
        P("section", None, "rep"),
        P("section", "rep", None),
        P("section", None, None),
    )
    out_specs = (P("section", "rep", None), P("section", "rep", None), P("section", "rep", None))
    return jax.shard_map(
        per_device, mesh=mesh, in_specs=in_specs, out_specs=out_specs, check_vma=False
    )
```

```python
import functools

import jax
import jax.numpy as jnp
from jax import lax
from jax.experimental import pallas as pl
from jax.experimental.pallas import tpu as pltpu
from jax.sharding import PartitionSpec as P

BLK = 2
NZ = 4
NY = 4
NC = 2

epsilon = 1e-05
step_rate = 0.5

F32 = jnp.float32
BF16 = jnp.bfloat16
WIDTH = 1024
VMEM_LIMIT = 40 << 20


def send(value, ds=0, dz=0, dy=0, dc=0):
    sections = lax.axis_size("section")
    replicas = lax.axis_size("rep")
    pairs = []
    for s in range(sections):
        for z in range(NZ):
            for y in range(NY):
                for c in range(NC):
                    source = s * replicas + (z * NY + y) * NC + c
                    target = (
                        ((s + ds) % sections) * replicas
                        + ((z ^ dz) * NY + (y + dy) % NY) * NC
                        + (c ^ dc)
                    )
                    pairs.append((source, target))
    return lax.ppermute(value, ("section", "rep"), pairs)


def group_at(index):
    me = lax.axis_index("rep")
    z, y, c = me // (NY * NC), (me // NC) % NY, me % NC
    dz, dy, dc = index % NZ, (index // NZ) % NY, index // (NZ * NY)
    return ((z ^ dz) * NY + (y + dy) % NY) * NC + (c ^ dc)


def selection(wiring, blocks_dev, capacity):
    groups = wiring.shape[0]
    per_group = blocks_dev * BLK
    per_slots = capacity * BLK
    per_unit = per_slots + per_group
    rows, columns = groups * per_group, groups * per_unit
    counts = wiring.astype(BF16)
    row_id = lax.broadcasted_iota(jnp.int32, (rows, groups), 0)
    row_member = lax.broadcasted_iota(jnp.int32, (rows, groups), 1)
    row_group = group_at(row_id // per_group)
    left = jnp.concatenate(
        [(row_member == row_group).astype(BF16), (row_member < row_group).astype(BF16)], axis=0
    )
    column_id = lax.broadcasted_iota(jnp.int32, (groups, columns), 1)
    column_member = lax.broadcasted_iota(jnp.int32, (groups, columns), 0)
    column_group = group_at(column_id // per_unit)
    right = jnp.concatenate(
        [(column_member == column_group).astype(BF16), (column_member < column_group).astype(BF16)],
        axis=1,
    )
    half = jnp.dot(left, counts, preferred_element_type=F32).astype(BF16)
    table = jnp.dot(half, right, preferred_element_type=F32).astype(jnp.int32)
    count = table[:rows, :columns]
    row_start = table[:rows, columns:]
    column_start = table[rows:, :columns]
    r = lax.broadcasted_iota(jnp.int32, (rows, columns), 0)
    q = lax.broadcasted_iota(jnp.int32, (rows, columns), 1)
    inner = q % per_unit
    block = (r % per_group) // BLK
    offset = block - row_start
    hit = (offset >= 0) & (offset < count) & (inner // BLK == column_start + offset)
    hit = hit & (inner < per_slots) & (r % BLK == inner % BLK)
    plain = (q // per_unit == r // per_group) & (inner == per_slots + r % per_group)
    chosen = jnp.concatenate([hit.astype(BF16), plain.astype(BF16)], axis=0)
    return lax.optimization_barrier(chosen)


def normalize(layer_rows, gain_row):
    values = layer_rows.astype(F32)
    row_scale = lax.rsqrt(jnp.mean(values * values, axis=1, keepdims=True) + epsilon)
    return values, row_scale, (values * row_scale * gain_row[None, :]).astype(BF16)


def dot(a, b, ca=1, cb=0):
    return lax.dot_general(a, b, (((ca,), (cb,)), ((), ())), preferred_element_type=F32)


def after(value, *others):
    return lax.optimization_barrier((value, *others))[0]


def add_up(parts):
    total = parts[0].astype(F32)
    for part in parts[1:]:
        total = total + part.astype(F32)
    return total


def cut(value, count):
    size = value.shape[0] // count
    return [value[i * size : (i + 1) * size] for i in range(count)]


def y_sum(terms):
    parts = cut(terms, NY)
    return add_up(
        [parts[0]] + [send(parts[k], dy=k) for k in range(1, NY)]
    ).astype(BF16)


def dot_t(a, b):
    return dot(a, b, 1, 1)


def first_kernel(count, *refs):
    select, spread = refs[:2]
    blocks = refs[2 : 2 + count]
    own_rows, gate_w, up_w, down_w = refs[2 + count : 6 + count]
    cot_out, normed_out, hidden_out, dgate_out, dup_out, mine, other = refs[6 + count : 13 + count]
    gate_sum, up_sum, dhidden_sum = refs[13 + count :]
    step, steps = pl.program_id(0), pl.num_programs(0) // 2
    tokens = dhidden_sum.shape[0]

    @pl.when(step < steps)
    def _():
        chosen = dot(select[...], jnp.concatenate([r[...] for r in blocks], axis=0)).astype(BF16)
        cotangent, normed = chosen[:tokens], chosen[tokens:]
        cot_out[...] = cotangent
        normed_out[...] = normed
        first = step == 0
        gate_sum[...] = jnp.where(first, 0.0, gate_sum[...]) + dot_t(normed, gate_w[...])
        up_sum[...] = jnp.where(first, 0.0, up_sum[...]) + dot_t(normed, up_w[...])
        dhidden_sum[...] = jnp.where(first, 0.0, dhidden_sum[...]) + dot_t(cotangent, down_w[...])

    @pl.when(step == steps - 1)
    def _():
        gate_act, up_act, grad = gate_sum[...], up_sum[...], dhidden_sum[...]
        sigmoid_gate = jax.nn.sigmoid(gate_act)
        silu_gate = gate_act * sigmoid_gate
        hidden_out[...] = (silu_gate * up_act).astype(BF16)
        dgate_out[...] = (
            grad * up_act * sigmoid_gate * (1.0 + gate_act * (1.0 - sigmoid_gate))
        ).astype(BF16)
        dup_out[...] = (grad * silu_gate).astype(BF16)

    @pl.when(step >= steps)
    def _():
        top = own_rows.shape[0]
        term = dot(hidden_out[...], down_w[...])
        term = jnp.concatenate([term[:top] + own_rows[...], term[top:]], axis=0)
        dterm = dot(dgate_out[...], gate_w[...]) + dot(dup_out[...], up_w[...])
        both = jnp.concatenate([term.astype(BF16), dterm.astype(BF16)], axis=0)
        terms = dot(spread[...], both).astype(BF16)
        mine[...] = terms[: mine.shape[0]]
        other[...] = terms[mine.shape[0] :]


def second_kernel(count, factor, *refs):
    nexts = refs[:count]
    normed, dgate, dup, gate_w, up_w = refs[count : 5 + count]
    gate_out, up_out, gate_sent, up_sent, gate_sum, up_sum, inner_sum = refs[5 + count :]
    first = pl.program_id(0) == 0
    rows = jnp.concatenate([r[...] for r in nexts], axis=0)
    gate_sum[...] = jnp.where(first, 0.0, gate_sum[...]) + dot_t(rows, gate_w[...])
    up_sum[...] = jnp.where(first, 0.0, up_sum[...]) + dot_t(rows, up_w[...])
    inner_sum[...] = jnp.where(first, 0.0, inner_sum[...]) + dot_t(rows, normed[...])

    @pl.when(pl.program_id(0) == pl.num_programs(0) - 1)
    def _():
        overlap = (-factor * inner_sum[...]).astype(BF16)
        gate_next = gate_sum[...] + dot(overlap, dgate[...])
        up_next = up_sum[...] + dot(overlap, dup[...])
        gate_out[...] = gate_next
        up_out[...] = up_next
        gate_sent[...] = gate_next.astype(BF16)
        up_sent[...] = up_next.astype(BF16)


def third_kernel(
    factor, row_count, gate, up, mate_gate, mate_up, hidden, cotangent, down_w, mine, other, hidden_next, overlap
):
    @pl.when(pl.program_id(0) == 0)
    def _():
        gate_next = 0.5 * (gate[...] + mate_gate[...].astype(F32))
        up_next = 0.5 * (up[...] + mate_up[...].astype(F32))
        units = (gate_next * jax.nn.sigmoid(gate_next) * up_next).astype(BF16)
        rows = units.shape[0]
        to = lax.broadcasted_iota(jnp.int32, (rows, rows), 0)
        at = lax.broadcasted_iota(jnp.int32, (rows, rows), 1)
        i, j = to & (row_count - 1), to // row_count
        z, replica, y, core = j & (NZ - 1), (j // NZ) & 1, (j // (2 * NZ)) & (NY - 1), j // (2 * NZ * NY)
        source = (((core * 2 + z // 2) * NY + y) * 2 + (z & 1)) * 2 + replica
        source = source * row_count + i
        order = jnp.where(at == source, 1.0, 0.0).astype(BF16)
        units = dot(order, units).astype(BF16)
        hidden_next[...] = units
        overlap[...] = (-factor * dot_t(units, hidden[...])).astype(BF16)

    term = dot(hidden_next[...], down_w[...]) + dot(overlap[...], cotangent[...])
    term = (0.5 * term).astype(BF16)
    mine[...] = term[: mine.shape[0]]
    other[...] = term[mine.shape[0] :]


def whole(shape):
    return pl.BlockSpec(shape, lambda i: (0,) * len(shape))


def columns(rows, width, at=lambda i: i):
    return pl.BlockSpec((rows, width), lambda i: (0, at(i)))


def run(kernel, steps, in_specs, outs, out_specs, scratch, flops, name, args):
    moved = sum(a.size * a.dtype.itemsize for a in args)
    return pl.pallas_call(
        kernel,
        grid=(steps,),
        in_specs=in_specs,
        out_shape=outs,
        out_specs=out_specs,
        scratch_shapes=scratch,
        cost_estimate=pl.CostEstimate(flops=flops, bytes_accessed=moved, transcendentals=0),
        compiler_params=pltpu.CompilerParams(vmem_limit_bytes=VMEM_LIMIT),
        name=name,
    )(*args)


def per_device(layer_in, next_in, returned, norm_gain, gate_weight, up_weight, down_weight, wiring):
    half_ring = lax.axis_size("section") // 2
    first_half = lax.axis_index("section") < half_ring
    row_count = layer_in.shape[1]
    blocks_dev = row_count // BLK
    capacity = returned.shape[1] // BLK
    token_count = row_count * lax.axis_size("rep")
    gain_row = norm_gain[0]
    gate_local, up_local, down_local = gate_weight[0].T, up_weight[0].T, down_weight[0]
    slot_rows = returned[0]

    update_factor = step_rate / token_count
    width = layer_in.shape[2]
    units = gate_local.shape[0]
    chunk = min(WIDTH, width)
    steps = width // chunk

    shifted = send(slot_rows, ds=-1)
    next_values, _, next_normed = normalize(next_in[0], gain_row)
    mate_normed = send(next_normed, ds=half_ring)
    values, row_scale, normed = normalize(layer_in[0], gain_row)
    select = selection(wiring[0], blocks_dev, capacity)
    spread = lax.optimization_barrier(select.T)

    next_y = jnp.concatenate(
        [
            jnp.where(first_half, next_normed, mate_normed),
            jnp.where(first_half, mate_normed, next_normed),
        ],
        axis=0,
    )
    next_y = jnp.concatenate([next_y, send(next_y, dz=1)], axis=0)
    next_z = jnp.concatenate([next_y] + [send(next_y, dy=-k) for k in range(1, NY)], axis=0)
    block_z = jnp.concatenate([shifted, normed], axis=0)
    block_y = jnp.concatenate(
        [block_z] + [send(block_z, dz=k) for k in range(1, NZ)], axis=0
    )
    block_y, next_z = lax.optimization_barrier((block_y, next_z))
    blocks = [block_y] + [send(block_y, dy=-k) for k in range(1, NY)]
    blocks = blocks + [send(block, dc=1) for block in blocks]
    nexts = [next_z, send(next_z, dz=2)]
    select, *nexts = lax.optimization_barrier((select, *nexts))
    nexts = nexts + [send(block, dc=1) for block in nexts]

    pair_tokens = 2 * token_count
    part = jax.ShapeDtypeStruct((token_count, units), BF16)
    product = jax.ShapeDtypeStruct((pair_tokens, units), F32)
    product_sent = jax.ShapeDtypeStruct((pair_tokens, units), BF16)
    rows = jax.ShapeDtypeStruct((token_count, width), BF16)
    half = jax.ShapeDtypeStruct((spread.shape[0] // NC, width), BF16)
    per_row = 2 * width * units
    own_rows = jnp.concatenate([values, jnp.zeros_like(values)], axis=0)

    def up_to(i):
        return jnp.minimum(i, steps - 1)

    def back(i):
        return steps - 1 - jnp.maximum(i - steps, 0)

    def there_and_back(i):
        return jnp.minimum(i, 2 * steps - 1 - i)

    cotangent, normed_all, hidden, grad_gate_act, grad_up_act, mine, other = run(
        functools.partial(first_kernel, len(blocks)),
        2 * steps,
        [whole(select.shape), whole(spread.shape)]
        + [columns(block.shape[0], chunk, up_to) for block in blocks]
        + [columns(own_rows.shape[0], chunk, back)]
        + [columns(units, chunk, there_and_back)] * 3,
        [rows, rows, part, part, part, half, half],
        [columns(token_count, chunk, up_to)] * 2
        + [whole(part.shape)] * 3
        + [columns(half.shape[0], chunk, back)] * 2,
        [pltpu.VMEM((token_count, units), F32)] * 3,
        per_row * token_count * 9,
        "first",
        [select, spread] + blocks + [own_rows, gate_local, up_local, down_local],
    )
    from_core = send(other, dc=1)
    gate_part, up_part, gate_sent, up_sent = run(
        functools.partial(second_kernel, len(nexts), update_factor),
        steps,
        [columns(block.shape[0], chunk) for block in nexts]
        + [columns(token_count, chunk), whole(part.shape), whole(part.shape)]
        + [columns(units, chunk)] * 2,
        [product, product, product_sent, product_sent],
        [whole(product.shape)] * 4,
        [
            pltpu.VMEM((pair_tokens, units), F32),
            pltpu.VMEM((pair_tokens, units), F32),
            pltpu.VMEM((pair_tokens, token_count), F32),
        ],
        per_row * token_count * 5,
        "second",
        nexts + [normed_all, grad_gate_act, grad_up_act, gate_local, up_local],
    )
    mate_gate = send(gate_sent, ds=half_ring)
    mate_up = send(up_sent, ds=half_ring)
    both = add_up([mine, after(from_core, gate_sent, up_sent)]).astype(BF16)
    both = y_sum(both)
    gate_part, up_part, both = lax.optimization_barrier((gate_part, up_part, both))

    half = jax.ShapeDtypeStruct((pair_tokens // NC, width), BF16)
    mine, other = run(
        functools.partial(third_kernel, update_factor, row_count),
        steps,
        [whole(product.shape)] * 4
        + [whole(part.shape), columns(token_count, chunk), columns(units, chunk)],
        [half, half],
        [columns(half.shape[0], chunk)] * 2,
        [pltpu.VMEM((pair_tokens, units), BF16), pltpu.VMEM((pair_tokens, token_count), BF16)],
        per_row * token_count * 3,
        "third",
        [gate_part, up_part, mate_gate, mate_up, hidden, cotangent, down_local],
    )
    pair = add_up([mine, send(other, dc=1)]).astype(BF16)
    both = cut(after(both, pair), NZ)
    both = add_up([both[0]] + [send(both[k], dz=k) for k in range(1, NZ)])
    forwarded = send(both[: slot_rows.shape[0]].astype(BF16), ds=1)
    dnormed = both[slot_rows.shape[0] :]
    first, second = cut(after(y_sum(pair), both), 2)
    own_part = jnp.where(first_half, first, second)
    mate_part = jnp.where(first_half, second, first)
    pair_sum = add_up([own_part, send(mate_part, ds=half_ring)]).astype(BF16)
    nparts = cut(pair_sum, NZ)
    next_out = add_up(
        [next_values, nparts[0]] + [send(nparts[k], dz=k) for k in range(1, NZ)]
    ).astype(BF16)
    scaled_grad = gain_row[None, :] * dnormed
    input_grad = (
        cotangent[:row_count].astype(F32)
        + row_scale * scaled_grad
        - values * row_scale**3 * jnp.mean(values * scaled_grad, axis=1, keepdims=True)
    ).astype(BF16)
    return (forwarded[None], input_grad[None], next_out[None])


def solution(mesh):
    in_specs = (
        P("section", "rep", None),
        P("section", "rep", None),
        P("section", "rep", None),
        P("section", None),
        P("section", None, "rep"),
        P("section", None, "rep"),
        P("section", "rep", None),
        P("section", None, None),
    )
    out_specs = (P("section", "rep", None), P("section", "rep", None), P("section", "rep", None))
    return jax.shard_map(
        per_device, mesh=mesh, in_specs=in_specs, out_specs=out_specs, check_vma=False
    )
```

```python
import functools

import jax
import jax.numpy as jnp
from jax import lax
from jax.experimental import pallas as pl
from jax.experimental.pallas import tpu as pltpu
from jax.sharding import PartitionSpec as P

BLK = 2
NZ = 4
NY = 4
NC = 2

epsilon = 1e-05
step_rate = 0.5

F32 = jnp.float32
BF16 = jnp.bfloat16
WIDTH = 1024
VMEM_LIMIT = 16 << 20


def send(value, ds=0, dz=0, dy=0, dc=0):
    sections = lax.axis_size("section")
    replicas = lax.axis_size("rep")
    pairs = []
    for s in range(sections):
        for z in range(NZ):
            for y in range(NY):
                for c in range(NC):
                    source = s * replicas + (z * NY + y) * NC + c
                    target = (
                        ((s + ds) % sections) * replicas
                        + ((z ^ dz) * NY + (y + dy) % NY) * NC
                        + (c ^ dc)
                    )
                    pairs.append((source, target))
    return lax.ppermute(value, ("section", "rep"), pairs)


def group_at(index):
    me = lax.axis_index("rep")
    z, y, c = me // (NY * NC), (me // NC) % NY, me % NC
    dz, dy, dc = index % NZ, (index // NZ) % NY, index // (NZ * NY)
    return ((z ^ dz) * NY + (y + dy) % NY) * NC + (c ^ dc)


def selection(wiring, blocks_dev, capacity):
    groups = wiring.shape[0]
    per_group = blocks_dev * BLK
    per_slots = capacity * BLK
    per_unit = per_slots + per_group
    rows, columns = groups * per_group, groups * per_unit
    counts = wiring.astype(BF16)
    row_id = lax.broadcasted_iota(jnp.int32, (rows, groups), 0)
    row_member = lax.broadcasted_iota(jnp.int32, (rows, groups), 1)
    row_group = group_at(row_id // per_group)
    left = jnp.concatenate(
        [(row_member == row_group).astype(BF16), (row_member < row_group).astype(BF16)], axis=0
    )
    column_id = lax.broadcasted_iota(jnp.int32, (groups, columns), 1)
    column_member = lax.broadcasted_iota(jnp.int32, (groups, columns), 0)
    column_group = group_at(column_id // per_unit)
    right = jnp.concatenate(
        [(column_member == column_group).astype(BF16), (column_member < column_group).astype(BF16)],
        axis=1,
    )
    half = jnp.dot(left, counts, preferred_element_type=F32).astype(BF16)
    table = jnp.dot(half, right, preferred_element_type=F32).astype(jnp.int32)
    count = table[:rows, :columns]
    row_start = table[:rows, columns:]
    column_start = table[rows:, :columns]
    r = lax.broadcasted_iota(jnp.int32, (rows, columns), 0)
    q = lax.broadcasted_iota(jnp.int32, (rows, columns), 1)
    inner = q % per_unit
    block = (r % per_group) // BLK
    offset = block - row_start
    hit = (offset >= 0) & (offset < count) & (inner // BLK == column_start + offset)
    hit = hit & (inner < per_slots) & (r % BLK == inner % BLK)
    plain = (q // per_unit == r // per_group) & (inner == per_slots + r % per_group)
    chosen = jnp.concatenate([hit.astype(BF16), plain.astype(BF16)], axis=0)
    return lax.optimization_barrier(chosen)


def normalize(layer_rows, gain_row):
    values = layer_rows.astype(F32)
    row_scale = lax.rsqrt(jnp.mean(values * values, axis=1, keepdims=True) + epsilon)
    return values, row_scale, (values * row_scale * gain_row[None, :]).astype(BF16)


def dot(a, b, ca=1, cb=0):
    return lax.dot_general(a, b, (((ca,), (cb,)), ((), ())), preferred_element_type=F32)


def after(value, *others):
    return lax.optimization_barrier((value, *others))[0]


def add_up(parts):
    total = parts[0].astype(F32)
    for part in parts[1:]:
        total = total + part.astype(F32)
    return total


def cut(value, count):
    size = value.shape[0] // count
    return [value[i * size : (i + 1) * size] for i in range(count)]


def y_sum(terms):
    parts = cut(terms, NY)
    return add_up(
        [parts[0]] + [send(parts[k], dy=k) for k in range(1, NY)]
    ).astype(BF16)


def dot_t(a, b):
    return dot(a, b, 1, 1)


def first_kernel(count, *refs):
    select, blocks = refs[0], refs[1 : 1 + count]
    gate_w, up_w, down_w = refs[1 + count : 4 + count]
    cot_out, normed_out, hidden_out, dgate_out, dup_out = refs[4 + count : 9 + count]
    gate_sum, up_sum, dhidden_sum = refs[9 + count :]
    tokens = dhidden_sum.shape[0]
    chosen = dot(select[...], jnp.concatenate([r[...] for r in blocks], axis=0)).astype(BF16)
    cotangent, normed = chosen[:tokens], chosen[tokens:]
    cot_out[...] = cotangent
    normed_out[...] = normed
    first = pl.program_id(0) == 0
    gate_sum[...] = jnp.where(first, 0.0, gate_sum[...]) + dot_t(normed, gate_w[...])
    up_sum[...] = jnp.where(first, 0.0, up_sum[...]) + dot_t(normed, up_w[...])
    dhidden_sum[...] = jnp.where(first, 0.0, dhidden_sum[...]) + dot_t(cotangent, down_w[...])

    @pl.when(pl.program_id(0) == pl.num_programs(0) - 1)
    def _():
        gate_act, up_act, grad = gate_sum[...], up_sum[...], dhidden_sum[...]
        sigmoid_gate = jax.nn.sigmoid(gate_act)
        silu_gate = gate_act * sigmoid_gate
        hidden_out[...] = (silu_gate * up_act).astype(BF16)
        dgate_out[...] = (
            grad * up_act * sigmoid_gate * (1.0 + gate_act * (1.0 - sigmoid_gate))
        ).astype(BF16)
        dup_out[...] = (grad * silu_gate).astype(BF16)


def terms_kernel(spread, hidden, dgate, dup, own_rows, gate_w, up_w, down_w, mine, other):
    top = own_rows.shape[0]
    term = dot(hidden[...], down_w[...])
    term = jnp.concatenate([term[:top] + own_rows[...], term[top:]], axis=0)
    dterm = dot(dgate[...], gate_w[...]) + dot(dup[...], up_w[...])
    both = jnp.concatenate([term.astype(BF16), dterm.astype(BF16)], axis=0)
    terms = dot(spread[...], both).astype(BF16)
    mine[...] = terms[: mine.shape[0]]
    other[...] = terms[mine.shape[0] :]


def second_kernel(count, factor, *refs):
    nexts = refs[:count]
    normed, dgate, dup, gate_w, up_w = refs[count : 5 + count]
    gate_out, up_out, gate_sent, up_sent, gate_sum, up_sum, inner_sum = refs[5 + count :]
    first = pl.program_id(0) == 0
    rows = jnp.concatenate([r[...] for r in nexts], axis=0)
    gate_sum[...] = jnp.where(first, 0.0, gate_sum[...]) + dot_t(rows, gate_w[...])
    up_sum[...] = jnp.where(first, 0.0, up_sum[...]) + dot_t(rows, up_w[...])
    inner_sum[...] = jnp.where(first, 0.0, inner_sum[...]) + dot_t(rows, normed[...])

    @pl.when(pl.program_id(0) == pl.num_programs(0) - 1)
    def _():
        overlap = (-factor * inner_sum[...]).astype(BF16)
        gate_next = gate_sum[...] + dot(overlap, dgate[...])
        up_next = up_sum[...] + dot(overlap, dup[...])
        gate_out[...] = gate_next
        up_out[...] = up_next
        gate_sent[...] = gate_next.astype(BF16)
        up_sent[...] = up_next.astype(BF16)


def third_kernel(
    factor, row_count, gate, up, mate_gate, mate_up, hidden, cotangent, down_w, mine, other, hidden_next, overlap
):
    @pl.when(pl.program_id(0) == 0)
    def _():
        gate_next = 0.5 * (gate[...] + mate_gate[...].astype(F32))
        up_next = 0.5 * (up[...] + mate_up[...].astype(F32))
        units = (gate_next * jax.nn.sigmoid(gate_next) * up_next).astype(BF16)
        rows = units.shape[0]
        to = lax.broadcasted_iota(jnp.int32, (rows, rows), 0)
        at = lax.broadcasted_iota(jnp.int32, (rows, rows), 1)
        i, j = to & (row_count - 1), to // row_count
        z, replica, y, core = j & (NZ - 1), (j // NZ) & 1, (j // (2 * NZ)) & (NY - 1), j // (2 * NZ * NY)
        source = (((core * 2 + z // 2) * NY + y) * 2 + (z & 1)) * 2 + replica
        source = source * row_count + i
        order = jnp.where(at == source, 1.0, 0.0).astype(BF16)
        units = dot(order, units).astype(BF16)
        hidden_next[...] = units
        overlap[...] = (-factor * dot_t(units, hidden[...])).astype(BF16)

    term = dot(hidden_next[...], down_w[...]) + dot(overlap[...], cotangent[...])
    term = (0.5 * term).astype(BF16)
    mine[...] = term[: mine.shape[0]]
    other[...] = term[mine.shape[0] :]


def whole(shape):
    return pl.BlockSpec(shape, lambda i: (0,) * len(shape))


def columns(rows, width, at=lambda i: i):
    return pl.BlockSpec((rows, width), lambda i: (0, at(i)))


def run(kernel, steps, in_specs, outs, out_specs, scratch, flops, name, args):
    moved = sum(a.size * a.dtype.itemsize for a in args)
    return pl.pallas_call(
        kernel,
        grid=(steps,),
        in_specs=in_specs,
        out_shape=outs,
        out_specs=out_specs,
        scratch_shapes=scratch,
        cost_estimate=pl.CostEstimate(flops=flops, bytes_accessed=moved, transcendentals=0),
        compiler_params=pltpu.CompilerParams(vmem_limit_bytes=VMEM_LIMIT),
        name=name,
    )(*args)


def per_device(layer_in, next_in, returned, norm_gain, gate_weight, up_weight, down_weight, wiring):
    half_ring = lax.axis_size("section") // 2
    first_half = lax.axis_index("section") < half_ring
    row_count = layer_in.shape[1]
    blocks_dev = row_count // BLK
    capacity = returned.shape[1] // BLK
    token_count = row_count * lax.axis_size("rep")
    gain_row = norm_gain[0]
    gate_local, up_local, down_local = [
        pltpu.with_memory_space_constraint(w, pltpu.HBM)
        for w in (gate_weight[0].T, up_weight[0].T, down_weight[0])
    ]
    slot_rows = returned[0]

    update_factor = step_rate / token_count
    width = layer_in.shape[2]
    units = gate_local.shape[0]
    chunk = min(WIDTH, width)
    steps = width // chunk

    shifted = send(slot_rows, ds=-1)
    next_values, _, next_normed = normalize(next_in[0], gain_row)
    mate_normed = send(next_normed, ds=half_ring)
    values, row_scale, normed = normalize(layer_in[0], gain_row)
    select = selection(wiring[0], blocks_dev, capacity)
    spread = lax.optimization_barrier(select.T)

    next_y = jnp.concatenate(
        [
            jnp.where(first_half, next_normed, mate_normed),
            jnp.where(first_half, mate_normed, next_normed),
        ],
        axis=0,
    )
    next_y = after(next_y, shifted)
    next_y = jnp.concatenate([next_y, send(next_y, dz=1)], axis=0)
    next_z = jnp.concatenate([next_y] + [send(next_y, dy=-k) for k in range(1, NY)], axis=0)
    block_z = jnp.concatenate([shifted, normed], axis=0)
    block_y = jnp.concatenate(
        [block_z] + [send(block_z, dz=k) for k in range(1, NZ)], axis=0
    )
    block_y, next_z = lax.optimization_barrier((block_y, next_z))
    blocks = [block_y] + [send(block_y, dy=-k) for k in range(1, NY)]
    blocks = blocks + [send(block, dc=1) for block in blocks]
    nexts = [next_z, send(next_z, dz=2)]

    pair_tokens = 2 * token_count
    part = jax.ShapeDtypeStruct((token_count, units), BF16)
    product = jax.ShapeDtypeStruct((pair_tokens, units), F32)
    product_sent = jax.ShapeDtypeStruct((pair_tokens, units), BF16)
    rows = jax.ShapeDtypeStruct((token_count, width), BF16)
    half = jax.ShapeDtypeStruct((spread.shape[0] // NC, width), BF16)
    per_row = 2 * width * units
    own_rows = jnp.concatenate([values, jnp.zeros_like(values)], axis=0)

    cotangent, normed_all, hidden, grad_gate_act, grad_up_act = run(
        functools.partial(first_kernel, len(blocks)),
        steps,
        [whole(select.shape)]
        + [columns(block.shape[0], chunk) for block in blocks]
        + [columns(units, chunk)] * 3,
        [rows, rows, part, part, part],
        [columns(token_count, chunk)] * 2 + [whole(part.shape)] * 3,
        [pltpu.VMEM((token_count, units), F32)] * 3,
        per_row * token_count * 4,
        "first",
        [select] + blocks + [gate_local, up_local, down_local],
    )
    nexts = nexts + [send(block, dc=1) for block in nexts]
    spread, *nexts = lax.optimization_barrier((spread, *nexts))
    mine, other = run(
        terms_kernel,
        steps,
        [whole(spread.shape)]
        + [whole(part.shape)] * 3
        + [columns(own_rows.shape[0], chunk)]
        + [columns(units, chunk)] * 3,
        [half, half],
        [columns(half.shape[0], chunk)] * 2,
        [],
        per_row * token_count * 5,
        "terms",
        [spread, hidden, grad_gate_act, grad_up_act, own_rows, gate_local, up_local, down_local],
    )
    from_core = send(other, dc=1)
    gate_part, up_part, gate_sent, up_sent = run(
        functools.partial(second_kernel, len(nexts), update_factor),
        steps,
        [columns(block.shape[0], chunk) for block in nexts]
        + [columns(token_count, chunk), whole(part.shape), whole(part.shape)]
        + [columns(units, chunk)] * 2,
        [product, product, product_sent, product_sent],
        [whole(product.shape)] * 4,
        [
            pltpu.VMEM((pair_tokens, units), F32),
            pltpu.VMEM((pair_tokens, units), F32),
            pltpu.VMEM((pair_tokens, token_count), F32),
        ],
        per_row * token_count * 5,
        "second",
        nexts + [normed_all, grad_gate_act, grad_up_act, gate_local, up_local],
    )
    mate_gate = send(gate_sent, ds=half_ring)
    mate_up = send(up_sent, ds=half_ring)
    both = add_up([mine, after(from_core, gate_sent, up_sent)]).astype(BF16)
    both = y_sum(both)
    gate_part, up_part, both = lax.optimization_barrier((gate_part, up_part, both))

    half = jax.ShapeDtypeStruct((pair_tokens // NC, width), BF16)
    mine, other = run(
        functools.partial(third_kernel, update_factor, row_count),
        steps,
        [whole(product.shape)] * 4
        + [whole(part.shape), columns(token_count, chunk), columns(units, chunk)],
        [half, half],
        [columns(half.shape[0], chunk)] * 2,
        [pltpu.VMEM((pair_tokens, units), BF16), pltpu.VMEM((pair_tokens, token_count), BF16)],
        per_row * token_count * 3,
        "third",
        [gate_part, up_part, mate_gate, mate_up, hidden, cotangent, down_local],
    )
    pair = add_up([mine, send(other, dc=1)]).astype(BF16)
    both = cut(after(both, pair), NZ)
    both = add_up([both[0]] + [send(both[k], dz=k) for k in range(1, NZ)])
    forwarded = send(both[: slot_rows.shape[0]].astype(BF16), ds=1)
    dnormed = both[slot_rows.shape[0] :]
    first, second = cut(after(y_sum(pair), both), 2)
    own_parts = cut(jnp.where(first_half, first, second), NZ)
    mate_parts = cut(jnp.where(first_half, second, first), NZ)
    next_out = add_up(
        [next_values, own_parts[0]]
        + [send(mate_parts[k], ds=half_ring, dz=k) for k in range(NZ)]
        + [send(own_parts[k], dz=k) for k in range(1, NZ)]
    ).astype(BF16)
    scaled_grad = gain_row[None, :] * dnormed
    input_grad = (
        cotangent[:row_count].astype(F32)
        + row_scale * scaled_grad
        - values * row_scale**3 * jnp.mean(values * scaled_grad, axis=1, keepdims=True)
    ).astype(BF16)
    return (forwarded[None], input_grad[None], next_out[None])


def solution(mesh):
    in_specs = (
        P("section", "rep", None),
        P("section", "rep", None),
        P("section", "rep", None),
        P("section", None),
        P("section", None, "rep"),
        P("section", None, "rep"),
        P("section", "rep", None),
        P("section", None, None),
    )
    out_specs = (P("section", "rep", None), P("section", "rep", None), P("section", "rep", None))
    return jax.shard_map(
        per_device, mesh=mesh, in_specs=in_specs, out_specs=out_specs, check_vma=False
    )
```

```python
import functools

import jax
import jax.numpy as jnp
from jax import lax
from jax.experimental import pallas as pl
from jax.experimental.pallas import tpu as pltpu
from jax.sharding import PartitionSpec as P

BLK = 2
NZ = 4
NY = 4
NC = 2

epsilon = 1e-05
step_rate = 0.5

F32 = jnp.float32
BF16 = jnp.bfloat16
WIDTH = 1024
VMEM_LIMIT = 16 << 20


def send(value, ds=0, dz=0, dy=0, dc=0):
    sections = lax.axis_size("section")
    replicas = lax.axis_size("rep")
    pairs = []
    for s in range(sections):
        for z in range(NZ):
            for y in range(NY):
                for c in range(NC):
                    source = s * replicas + (z * NY + y) * NC + c
                    target = (
                        ((s + ds) % sections) * replicas
                        + ((z ^ dz) * NY + (y + dy) % NY) * NC
                        + (c ^ dc)
                    )
                    pairs.append((source, target))
    return lax.ppermute(value, ("section", "rep"), pairs)


def group_at(index):
    me = lax.axis_index("rep")
    z, y, c = me // (NY * NC), (me // NC) % NY, me % NC
    dz, dy, dc = index % NZ, (index // NZ) % NY, index // (NZ * NY)
    return ((z ^ dz) * NY + (y + dy) % NY) * NC + (c ^ dc)


def selection(wiring, blocks_dev, capacity):
    groups = wiring.shape[0]
    per_group = blocks_dev * BLK
    per_slots = capacity * BLK
    per_unit = per_slots + per_group
    rows, columns = groups * per_group, groups * per_unit
    counts = wiring.astype(BF16)
    row_id = lax.broadcasted_iota(jnp.int32, (rows, groups), 0)
    row_member = lax.broadcasted_iota(jnp.int32, (rows, groups), 1)
    row_group = group_at(row_id // per_group)
    left = jnp.concatenate(
        [(row_member == row_group).astype(BF16), (row_member < row_group).astype(BF16)], axis=0
    )
    column_id = lax.broadcasted_iota(jnp.int32, (groups, columns), 1)
    column_member = lax.broadcasted_iota(jnp.int32, (groups, columns), 0)
    column_group = group_at(column_id // per_unit)
    right = jnp.concatenate(
        [(column_member == column_group).astype(BF16), (column_member < column_group).astype(BF16)],
        axis=1,
    )
    half = jnp.dot(left, counts, preferred_element_type=F32).astype(BF16)
    table = jnp.dot(half, right, preferred_element_type=F32).astype(jnp.int32)
    count = table[:rows, :columns]
    row_start = table[:rows, columns:]
    column_start = table[rows:, :columns]
    r = lax.broadcasted_iota(jnp.int32, (rows, columns), 0)
    q = lax.broadcasted_iota(jnp.int32, (rows, columns), 1)
    inner = q % per_unit
    block = (r % per_group) // BLK
    offset = block - row_start
    hit = (offset >= 0) & (offset < count) & (inner // BLK == column_start + offset)
    hit = hit & (inner < per_slots) & (r % BLK == inner % BLK)
    plain = (q // per_unit == r // per_group) & (inner == per_slots + r % per_group)
    chosen = jnp.concatenate([hit.astype(BF16), plain.astype(BF16)], axis=0)
    return lax.optimization_barrier(chosen)


def normalize(layer_rows, gain_row):
    values = layer_rows.astype(F32)
    row_scale = lax.rsqrt(jnp.mean(values * values, axis=1, keepdims=True) + epsilon)
    return values, row_scale, (values * row_scale * gain_row[None, :]).astype(BF16)


def dot(a, b, ca=1, cb=0):
    return lax.dot_general(a, b, (((ca,), (cb,)), ((), ())), preferred_element_type=F32)


def after(value, *others):
    return lax.optimization_barrier((value, *others))[0]


def add_up(parts):
    total = parts[0].astype(F32)
    for part in parts[1:]:
        total = total + part.astype(F32)
    return total


def cut(value, count):
    size = value.shape[0] // count
    return [value[i * size : (i + 1) * size] for i in range(count)]


def y_sum(terms):
    parts = cut(terms, NY)
    return add_up(
        [parts[0]] + [send(parts[k], dy=k) for k in range(1, NY)]
    ).astype(BF16)


def dot_t(a, b):
    return dot(a, b, 1, 1)


def first_kernel(count, *refs):
    select, blocks = refs[0], refs[1 : 1 + count]
    gate_w, up_w, down_w = refs[1 + count : 4 + count]
    cot_out, normed_out, hidden_out, dgate_out, dup_out = refs[4 + count : 9 + count]
    gate_sum, up_sum, dhidden_sum = refs[9 + count :]
    tokens = dhidden_sum.shape[0]
    chosen = dot(select[...], jnp.concatenate([r[...] for r in blocks], axis=0)).astype(BF16)
    cotangent, normed = chosen[:tokens], chosen[tokens:]
    cot_out[...] = cotangent
    normed_out[...] = normed
    first = pl.program_id(0) == 0
    gate_sum[...] = jnp.where(first, 0.0, gate_sum[...]) + dot_t(normed, gate_w[...])
    up_sum[...] = jnp.where(first, 0.0, up_sum[...]) + dot_t(normed, up_w[...])
    dhidden_sum[...] = jnp.where(first, 0.0, dhidden_sum[...]) + dot_t(cotangent, down_w[...])

    @pl.when(pl.program_id(0) == pl.num_programs(0) - 1)
    def _():
        gate_act, up_act, grad = gate_sum[...], up_sum[...], dhidden_sum[...]
        sigmoid_gate = jax.nn.sigmoid(gate_act)
        silu_gate = gate_act * sigmoid_gate
        hidden_out[...] = (silu_gate * up_act).astype(BF16)
        dgate_out[...] = (
            grad * up_act * sigmoid_gate * (1.0 + gate_act * (1.0 - sigmoid_gate))
        ).astype(BF16)
        dup_out[...] = (grad * silu_gate).astype(BF16)


def terms_kernel(spread, hidden, dgate, dup, own_rows, gate_w, up_w, down_w, mine, other):
    top = own_rows.shape[0]
    term = dot(hidden[...], down_w[...])
    term = jnp.concatenate([term[:top] + own_rows[...], term[top:]], axis=0)
    dterm = dot(dgate[...], gate_w[...]) + dot(dup[...], up_w[...])
    both = jnp.concatenate([term.astype(BF16), dterm.astype(BF16)], axis=0)
    terms = dot(spread[...], both).astype(BF16)
    mine[...] = terms[: mine.shape[0]]
    other[...] = terms[mine.shape[0] :]


def second_kernel(count, factor, *refs):
    nexts = refs[:count]
    normed, dgate, dup, gate_w, up_w = refs[count : 5 + count]
    gate_out, up_out, sent, gate_sum, up_sum, inner_sum = refs[5 + count :]
    first = pl.program_id(0) == 0
    rows = jnp.concatenate([r[...] for r in nexts], axis=0)
    gate_sum[...] = jnp.where(first, 0.0, gate_sum[...]) + dot_t(rows, gate_w[...])
    up_sum[...] = jnp.where(first, 0.0, up_sum[...]) + dot_t(rows, up_w[...])
    inner_sum[...] = jnp.where(first, 0.0, inner_sum[...]) + dot_t(rows, normed[...])

    @pl.when(pl.program_id(0) == pl.num_programs(0) - 1)
    def _():
        overlap = (-factor * inner_sum[...]).astype(BF16)
        gate_next = gate_sum[...] + dot(overlap, dgate[...])
        up_next = up_sum[...] + dot(overlap, dup[...])
        gate_out[...] = gate_next
        up_out[...] = up_next
        sent[: gate_next.shape[0]] = gate_next.astype(BF16)
        sent[gate_next.shape[0] :] = up_next.astype(BF16)


def third_kernel(
    factor, row_count, gate, up, from_mate, hidden, cotangent, down_w, mine, other, hidden_next, overlap
):
    @pl.when(pl.program_id(0) == 0)
    def _():
        pairs = gate.shape[0]
        gate_next = 0.5 * (gate[...] + from_mate[:pairs].astype(F32))
        up_next = 0.5 * (up[...] + from_mate[pairs:].astype(F32))
        units = (gate_next * jax.nn.sigmoid(gate_next) * up_next).astype(BF16)
        rows = units.shape[0]
        to = lax.broadcasted_iota(jnp.int32, (rows, rows), 0)
        at = lax.broadcasted_iota(jnp.int32, (rows, rows), 1)
        i, j = to & (row_count - 1), to // row_count
        z, replica, y, core = j & (NZ - 1), (j // NZ) & 1, (j // (2 * NZ)) & (NY - 1), j // (2 * NZ * NY)
        source = (((core * NZ + z) * 2 + replica) * NY + y) * row_count + i
        order = jnp.where(at == source, 1.0, 0.0).astype(BF16)
        units = dot(order, units).astype(BF16)
        hidden_next[...] = units
        overlap[...] = (-factor * dot_t(units, hidden[...])).astype(BF16)

    term = dot(hidden_next[...], down_w[...]) + dot(overlap[...], cotangent[...])
    term = (0.5 * term).astype(BF16)
    mine[...] = term[: mine.shape[0]]
    other[...] = term[mine.shape[0] :]


def whole(shape):
    return pl.BlockSpec(shape, lambda i: (0,) * len(shape))


def columns(rows, width, at=lambda i: i):
    return pl.BlockSpec((rows, width), lambda i: (0, at(i)))


def run(kernel, steps, in_specs, outs, out_specs, scratch, flops, name, args):
    moved = sum(a.size * a.dtype.itemsize for a in args)
    return pl.pallas_call(
        kernel,
        grid=(steps,),
        in_specs=in_specs,
        out_shape=outs,
        out_specs=out_specs,
        scratch_shapes=scratch,
        cost_estimate=pl.CostEstimate(flops=flops, bytes_accessed=moved, transcendentals=0),
        compiler_params=pltpu.CompilerParams(vmem_limit_bytes=VMEM_LIMIT),
        name=name,
    )(*args)


def per_device(layer_in, next_in, returned, norm_gain, gate_weight, up_weight, down_weight, wiring):
    half_ring = lax.axis_size("section") // 2
    first_half = lax.axis_index("section") < half_ring
    row_count = layer_in.shape[1]
    blocks_dev = row_count // BLK
    capacity = returned.shape[1] // BLK
    token_count = row_count * lax.axis_size("rep")
    gain_row = norm_gain[0]
    gate_local, up_local, down_local = [
        pltpu.with_memory_space_constraint(w, pltpu.HBM)
        for w in (gate_weight[0].T, up_weight[0].T, down_weight[0])
    ]
    slot_rows = returned[0]

    update_factor = step_rate / token_count
    width = layer_in.shape[2]
    units = gate_local.shape[0]
    chunk = min(WIDTH, width)
    steps = width // chunk

    next_values, _, next_normed = normalize(next_in[0], gain_row)
    values, row_scale, normed = normalize(layer_in[0], gain_row)
    shifted = send(after(slot_rows, normed, next_normed), ds=-1)
    select = selection(wiring[0], blocks_dev, capacity)
    spread = lax.optimization_barrier(select.T)

    next_y = jnp.concatenate([next_normed] + [send(next_normed, dy=-k) for k in range(1, NY)], axis=0)
    mate_y = send(next_y, ds=half_ring)
    next_z = jnp.concatenate(
        [jnp.where(first_half, next_y, mate_y), jnp.where(first_half, mate_y, next_y)], axis=0
    )
    block_z = jnp.concatenate([shifted, normed], axis=0)
    block_y = jnp.concatenate(
        [block_z] + [send(block_z, dz=k) for k in range(1, NZ)], axis=0
    )
    block_y, next_z = lax.optimization_barrier((block_y, next_z))
    next_z = jnp.concatenate([next_z, send(next_z, dz=1)], axis=0)
    blocks = [block_y] + [send(block_y, dy=-k) for k in range(1, NY)]
    blocks = blocks + [send(block, dc=1) for block in blocks]
    nexts = [next_z, send(next_z, dz=2)]

    pair_tokens = 2 * token_count
    part = jax.ShapeDtypeStruct((token_count, units), BF16)
    product = jax.ShapeDtypeStruct((pair_tokens, units), F32)
    product_sent = jax.ShapeDtypeStruct((2 * pair_tokens, units), BF16)
    rows = jax.ShapeDtypeStruct((token_count, width), BF16)
    half = jax.ShapeDtypeStruct((spread.shape[0] // NC, width), BF16)
    per_row = 2 * width * units
    own_rows = jnp.concatenate([values, jnp.zeros_like(values)], axis=0)

    cotangent, normed_all, hidden, grad_gate_act, grad_up_act = run(
        functools.partial(first_kernel, len(blocks)),
        steps,
        [whole(select.shape)]
        + [columns(block.shape[0], chunk) for block in blocks]
        + [columns(units, chunk)] * 3,
        [rows, rows, part, part, part],
        [columns(token_count, chunk)] * 2 + [whole(part.shape)] * 3,
        [pltpu.VMEM((token_count, units), F32)] * 3,
        per_row * token_count * 4,
        "first",
        [select] + blocks + [gate_local, up_local, down_local],
    )
    nexts = nexts + [send(block, dc=1) for block in nexts]
    spread, *nexts = lax.optimization_barrier((spread, *nexts))
    mine, other = run(
        terms_kernel,
        steps,
        [whole(spread.shape)]
        + [whole(part.shape)] * 3
        + [columns(own_rows.shape[0], chunk)]
        + [columns(units, chunk)] * 3,
        [half, half],
        [columns(half.shape[0], chunk)] * 2,
        [],
        per_row * token_count * 5,
        "terms",
        [spread, hidden, grad_gate_act, grad_up_act, own_rows, gate_local, up_local, down_local],
    )
    from_core = send(other, dc=1)
    gate_part, up_part, sent = run(
        functools.partial(second_kernel, len(nexts), update_factor),
        steps,
        [columns(block.shape[0], chunk) for block in nexts]
        + [columns(token_count, chunk), whole(part.shape), whole(part.shape)]
        + [columns(units, chunk)] * 2,
        [product, product, product_sent],
        [whole(product.shape)] * 2 + [whole(product_sent.shape)],
        [
            pltpu.VMEM((pair_tokens, units), F32),
            pltpu.VMEM((pair_tokens, units), F32),
            pltpu.VMEM((pair_tokens, token_count), F32),
        ],
        per_row * token_count * 5,
        "second",
        nexts + [normed_all, grad_gate_act, grad_up_act, gate_local, up_local],
    )
    from_mate = send(sent, ds=half_ring)
    both = add_up([mine, after(from_core, sent)]).astype(BF16)
    both = y_sum(both)
    gate_part, up_part, both = lax.optimization_barrier((gate_part, up_part, both))

    half = jax.ShapeDtypeStruct((pair_tokens // NC, width), BF16)
    mine, other = run(
        functools.partial(third_kernel, update_factor, row_count),
        steps,
        [whole(product.shape)] * 2
        + [whole(product_sent.shape), whole(part.shape)]
        + [columns(token_count, chunk), columns(units, chunk)],
        [half, half],
        [columns(half.shape[0], chunk)] * 2,
        [pltpu.VMEM((pair_tokens, units), BF16), pltpu.VMEM((pair_tokens, token_count), BF16)],
        per_row * token_count * 3,
        "third",
        [gate_part, up_part, from_mate, hidden, cotangent, down_local],
    )
    pair = add_up([mine, send(other, dc=1)]).astype(BF16)
    both = cut(after(both, pair), NZ)
    both = add_up([both[0]] + [send(both[k], dz=k) for k in range(1, NZ)])
    forwarded = send(both[: slot_rows.shape[0]].astype(BF16), ds=1)
    dnormed = both[slot_rows.shape[0] :]
    first, second = cut(after(y_sum(pair), both), 2)
    own_parts = cut(jnp.where(first_half, first, second), NZ)
    mate_parts = cut(jnp.where(first_half, second, first), NZ)
    next_out = add_up(
        [next_values, own_parts[0]]
        + [send(mate_parts[k], ds=half_ring, dz=k) for k in range(NZ)]
        + [send(own_parts[k], dz=k) for k in range(1, NZ)]
    ).astype(BF16)
    scaled_grad = gain_row[None, :] * dnormed
    input_grad = (
        cotangent[:row_count].astype(F32)
        + row_scale * scaled_grad
        - values * row_scale**3 * jnp.mean(values * scaled_grad, axis=1, keepdims=True)
    ).astype(BF16)
    return (forwarded[None], input_grad[None], next_out[None])


def solution(mesh):
    in_specs = (
        P("section", "rep", None),
        P("section", "rep", None),
        P("section", "rep", None),
        P("section", None),
        P("section", None, "rep"),
        P("section", None, "rep"),
        P("section", "rep", None),
        P("section", None, None),
    )
    out_specs = (P("section", "rep", None), P("section", "rep", None), P("section", "rep", None))
    return jax.shard_map(
        per_device, mesh=mesh, in_specs=in_specs, out_specs=out_specs, check_vma=False
    )
```

```python
import functools

import jax
import jax.numpy as jnp
from jax import lax
from jax.experimental import pallas as pl
from jax.experimental.pallas import tpu as pltpu
from jax.sharding import PartitionSpec as P

BLK = 2
NZ = 4
NY = 4
NC = 2

epsilon = 1e-05
step_rate = 0.5

F32 = jnp.float32
BF16 = jnp.bfloat16
WIDTH = 1024
VMEM_LIMIT = 16 << 20


def send(value, ds=0, dz=0, dy=0, dc=0):
    sections = lax.axis_size("section")
    replicas = lax.axis_size("rep")
    pairs = []
    for s in range(sections):
        for z in range(NZ):
            for y in range(NY):
                for c in range(NC):
                    source = s * replicas + (z * NY + y) * NC + c
                    target = (
                        ((s + ds) % sections) * replicas
                        + ((z ^ dz) * NY + (y + dy) % NY) * NC
                        + (c ^ dc)
                    )
                    pairs.append((source, target))
    return lax.ppermute(value, ("section", "rep"), pairs)


def group_at(index):
    me = lax.axis_index("rep")
    z, y, c = me // (NY * NC), (me // NC) % NY, me % NC
    dz, dy, dc = index % NZ, (index // NZ) % NY, index // (NZ * NY)
    return ((z ^ dz) * NY + (y + dy) % NY) * NC + (c ^ dc)


def selection(wiring, blocks_dev, capacity):
    groups = wiring.shape[0]
    per_group = blocks_dev * BLK
    per_slots = capacity * BLK
    per_unit = per_slots + per_group
    rows, columns = groups * per_group, groups * per_unit
    counts = wiring.astype(BF16)
    row_id = lax.broadcasted_iota(jnp.int32, (rows, groups), 0)
    row_member = lax.broadcasted_iota(jnp.int32, (rows, groups), 1)
    row_group = group_at(row_id // per_group)
    left = jnp.concatenate(
        [(row_member == row_group).astype(BF16), (row_member < row_group).astype(BF16)], axis=0
    )
    column_id = lax.broadcasted_iota(jnp.int32, (groups, columns), 1)
    column_member = lax.broadcasted_iota(jnp.int32, (groups, columns), 0)
    column_group = group_at(column_id // per_unit)
    right = jnp.concatenate(
        [(column_member == column_group).astype(BF16), (column_member < column_group).astype(BF16)],
        axis=1,
    )
    half = jnp.dot(left, counts, preferred_element_type=F32).astype(BF16)
    table = jnp.dot(half, right, preferred_element_type=F32).astype(jnp.int32)
    count = table[:rows, :columns]
    row_start = table[:rows, columns:]
    column_start = table[rows:, :columns]
    r = lax.broadcasted_iota(jnp.int32, (rows, columns), 0)
    q = lax.broadcasted_iota(jnp.int32, (rows, columns), 1)
    inner = q % per_unit
    block = (r % per_group) // BLK
    offset = block - row_start
    hit = (offset >= 0) & (offset < count) & (inner // BLK == column_start + offset)
    hit = hit & (inner < per_slots) & (r % BLK == inner % BLK)
    plain = (q // per_unit == r // per_group) & (inner == per_slots + r % per_group)
    chosen = jnp.concatenate([hit.astype(BF16), plain.astype(BF16)], axis=0)
    return lax.optimization_barrier(chosen)


def normalize(layer_rows, gain_row):
    values = layer_rows.astype(F32)
    row_scale = lax.rsqrt(jnp.mean(values * values, axis=1, keepdims=True) + epsilon)
    return values, row_scale, (values * row_scale * gain_row[None, :]).astype(BF16)


def dot(a, b, ca=1, cb=0):
    return lax.dot_general(a, b, (((ca,), (cb,)), ((), ())), preferred_element_type=F32)


def after(value, *others):
    return lax.optimization_barrier((value, *others))[0]


def add_up(parts):
    total = parts[0].astype(F32)
    for part in parts[1:]:
        total = total + part.astype(F32)
    return total


def cut(value, count):
    size = value.shape[0] // count
    return [value[i * size : (i + 1) * size] for i in range(count)]


def y_sum(terms):
    parts = cut(terms, NY)
    return add_up(
        [parts[0]] + [send(parts[k], dy=k) for k in range(1, NY)]
    ).astype(BF16)


def dot_t(a, b):
    return dot(a, b, 1, 1)


def first_kernel(count, *refs):
    select, blocks = refs[0], refs[1 : 1 + count]
    gate_w, up_w, down_w = refs[1 + count : 4 + count]
    cot_out, normed_out, hidden_out, dgate_out, dup_out = refs[4 + count : 9 + count]
    gate_sum, up_sum, dhidden_sum = refs[9 + count :]
    tokens = dhidden_sum.shape[0]
    chosen = dot(select[...], jnp.concatenate([r[...] for r in blocks], axis=0)).astype(BF16)
    cotangent, normed = chosen[:tokens], chosen[tokens:]
    cot_out[...] = cotangent
    normed_out[...] = normed
    first = pl.program_id(0) == 0
    gate_sum[...] = jnp.where(first, 0.0, gate_sum[...]) + dot_t(normed, gate_w[...])
    up_sum[...] = jnp.where(first, 0.0, up_sum[...]) + dot_t(normed, up_w[...])
    dhidden_sum[...] = jnp.where(first, 0.0, dhidden_sum[...]) + dot_t(cotangent, down_w[...])

    @pl.when(pl.program_id(0) == pl.num_programs(0) - 1)
    def _():
        gate_act, up_act, grad = gate_sum[...], up_sum[...], dhidden_sum[...]
        sigmoid_gate = jax.nn.sigmoid(gate_act)
        silu_gate = gate_act * sigmoid_gate
        hidden_out[...] = (silu_gate * up_act).astype(BF16)
        dgate_out[...] = (
            grad * up_act * sigmoid_gate * (1.0 + gate_act * (1.0 - sigmoid_gate))
        ).astype(BF16)
        dup_out[...] = (grad * silu_gate).astype(BF16)


def terms_kernel(spread, hidden, dgate, dup, own_rows, gate_w, up_w, down_w, mine, other):
    top = own_rows.shape[0]
    term = dot(hidden[...], down_w[...])
    term = jnp.concatenate([term[:top] + own_rows[...], term[top:]], axis=0)
    dterm = dot(dgate[...], gate_w[...]) + dot(dup[...], up_w[...])
    both = jnp.concatenate([term.astype(BF16), dterm.astype(BF16)], axis=0)
    terms = dot(spread[...], both).astype(BF16)
    mine[...] = terms[: mine.shape[0]]
    other[...] = terms[mine.shape[0] :]


def second_kernel(count, factor, *refs):
    nexts = refs[:count]
    normed, dgate, dup, gate_w, up_w = refs[count : 5 + count]
    gate_out, up_out, gate_sent, up_sent, gate_sum, up_sum, inner_sum = refs[5 + count :]
    first = pl.program_id(0) == 0
    rows = jnp.concatenate([r[...] for r in nexts], axis=0)
    gate_sum[...] = jnp.where(first, 0.0, gate_sum[...]) + dot_t(rows, gate_w[...])
    up_sum[...] = jnp.where(first, 0.0, up_sum[...]) + dot_t(rows, up_w[...])
    inner_sum[...] = jnp.where(first, 0.0, inner_sum[...]) + dot_t(rows, normed[...])

    @pl.when(pl.program_id(0) == pl.num_programs(0) - 1)
    def _():
        overlap = (-factor * inner_sum[...]).astype(BF16)
        gate_next = gate_sum[...] + dot(overlap, dgate[...])
        up_next = up_sum[...] + dot(overlap, dup[...])
        gate_out[...] = gate_next
        up_out[...] = up_next
        gate_sent[...] = gate_next.astype(BF16)
        up_sent[...] = up_next.astype(BF16)


def third_kernel(
    factor, row_count, gate, up, mate_gate, mate_up, hidden, cotangent, down_w, mine, other, hidden_next, overlap
):
    @pl.when(pl.program_id(0) == 0)
    def _():
        gate_next = 0.5 * (gate[...] + mate_gate[...].astype(F32))
        up_next = 0.5 * (up[...] + mate_up[...].astype(F32))
        units = (gate_next * jax.nn.sigmoid(gate_next) * up_next).astype(BF16)
        rows = units.shape[0]
        to = lax.broadcasted_iota(jnp.int32, (rows, rows), 0)
        at = lax.broadcasted_iota(jnp.int32, (rows, rows), 1)
        i, j = to & (row_count - 1), to // row_count
        z, replica, y, core = j & (NZ - 1), (j // NZ) & 1, (j // (2 * NZ)) & (NY - 1), j // (2 * NZ * NY)
        source = (((core * 2 + z // 2) * NY + y) * 2 + (z & 1)) * 2 + replica
        source = source * row_count + i
        order = jnp.where(at == source, 1.0, 0.0).astype(BF16)
        units = dot(order, units).astype(BF16)
        hidden_next[...] = units
        overlap[...] = (-factor * dot_t(units, hidden[...])).astype(BF16)

    term = dot(hidden_next[...], down_w[...]) + dot(overlap[...], cotangent[...])
    term = (0.5 * term).astype(BF16)
    mine[...] = term[: mine.shape[0]]
    other[...] = term[mine.shape[0] :]


def whole(shape):
    return pl.BlockSpec(shape, lambda i: (0,) * len(shape))


def columns(rows, width, at=lambda i: i):
    return pl.BlockSpec((rows, width), lambda i: (0, at(i)))


def run(kernel, steps, in_specs, outs, out_specs, scratch, flops, name, args):
    moved = sum(a.size * a.dtype.itemsize for a in args)
    return pl.pallas_call(
        kernel,
        grid=(steps,),
        in_specs=in_specs,
        out_shape=outs,
        out_specs=out_specs,
        scratch_shapes=scratch,
        cost_estimate=pl.CostEstimate(flops=flops, bytes_accessed=moved, transcendentals=0),
        compiler_params=pltpu.CompilerParams(vmem_limit_bytes=VMEM_LIMIT),
        name=name,
    )(*args)


def per_device(layer_in, next_in, returned, norm_gain, gate_weight, up_weight, down_weight, wiring):
    half_ring = lax.axis_size("section") // 2
    first_half = lax.axis_index("section") < half_ring
    row_count = layer_in.shape[1]
    blocks_dev = row_count // BLK
    capacity = returned.shape[1] // BLK
    token_count = row_count * lax.axis_size("rep")
    gain_row = norm_gain[0]
    gate_local, up_local, down_local = [
        pltpu.with_memory_space_constraint(w, pltpu.HBM)
        for w in (gate_weight[0].T, up_weight[0].T, down_weight[0])
    ]
    gate_near, up_near, down_near = [
        pltpu.with_memory_space_constraint(w, pltpu.VMEM)
        for w in (gate_weight[0].T, up_weight[0].T, down_weight[0])
    ]
    slot_rows = returned[0]

    update_factor = step_rate / token_count
    width = layer_in.shape[2]
    units = gate_local.shape[0]
    chunk = min(WIDTH, width)
    steps = width // chunk

    shifted = send(slot_rows, ds=-1)
    next_values, _, next_normed = normalize(next_in[0], gain_row)
    mate_normed = send(next_normed, ds=half_ring)
    values, row_scale, normed = normalize(layer_in[0], gain_row)
    select = selection(wiring[0], blocks_dev, capacity)
    spread = lax.optimization_barrier(select.T)

    next_y = jnp.concatenate(
        [
            jnp.where(first_half, next_normed, mate_normed),
            jnp.where(first_half, mate_normed, next_normed),
        ],
        axis=0,
    )
    next_y = after(next_y, shifted)
    next_y = jnp.concatenate([next_y, send(next_y, dz=1)], axis=0)
    next_z = jnp.concatenate([next_y] + [send(next_y, dy=-k) for k in range(1, NY)], axis=0)
    block_z = jnp.concatenate([shifted, normed], axis=0)
    block_y = jnp.concatenate(
        [block_z] + [send(block_z, dz=k) for k in range(1, NZ)], axis=0
    )
    block_y, next_z = lax.optimization_barrier((block_y, next_z))
    blocks = [block_y] + [send(block_y, dy=-k) for k in range(1, NY)]
    blocks = blocks + [send(block, dc=1) for block in blocks]
    nexts = [next_z, send(next_z, dz=2)]

    pair_tokens = 2 * token_count
    part = jax.ShapeDtypeStruct((token_count, units), BF16)
    product = jax.ShapeDtypeStruct((pair_tokens, units), F32)
    product_sent = jax.ShapeDtypeStruct((pair_tokens, units), BF16)
    rows = jax.ShapeDtypeStruct((token_count, width), BF16)
    half = jax.ShapeDtypeStruct((spread.shape[0] // NC, width), BF16)
    per_row = 2 * width * units
    own_rows = jnp.concatenate([values, jnp.zeros_like(values)], axis=0)

    cotangent, normed_all, hidden, grad_gate_act, grad_up_act = run(
        functools.partial(first_kernel, len(blocks)),
        steps,
        [whole(select.shape)]
        + [columns(block.shape[0], chunk) for block in blocks]
        + [columns(units, chunk)] * 3,
        [rows, rows, part, part, part],
        [columns(token_count, chunk)] * 2 + [whole(part.shape)] * 3,
        [pltpu.VMEM((token_count, units), F32)] * 3,
        per_row * token_count * 4,
        "first",
        [select] + blocks + [gate_local, up_local, down_local],
    )
    nexts = nexts + [send(block, dc=1) for block in nexts]
    spread, *nexts = lax.optimization_barrier((spread, *nexts))
    mine, other = run(
        terms_kernel,
        steps,
        [whole(spread.shape)]
        + [whole(part.shape)] * 3
        + [columns(own_rows.shape[0], chunk)]
        + [columns(units, chunk)] * 3,
        [half, half],
        [columns(half.shape[0], chunk)] * 2,
        [],
        per_row * token_count * 5,
        "terms",
        [spread, hidden, grad_gate_act, grad_up_act, own_rows, gate_near, up_near, down_near],
    )
    from_core = send(other, dc=1)
    gate_part, up_part, gate_sent, up_sent = run(
        functools.partial(second_kernel, len(nexts), update_factor),
        steps,
        [columns(block.shape[0], chunk) for block in nexts]
        + [columns(token_count, chunk), whole(part.shape), whole(part.shape)]
        + [columns(units, chunk)] * 2,
        [product, product, product_sent, product_sent],
        [whole(product.shape)] * 4,
        [
            pltpu.VMEM((pair_tokens, units), F32),
            pltpu.VMEM((pair_tokens, units), F32),
            pltpu.VMEM((pair_tokens, token_count), F32),
        ],
        per_row * token_count * 5,
        "second",
        nexts + [normed_all, grad_gate_act, grad_up_act, gate_near, up_near],
    )
    mate_gate = send(gate_sent, ds=half_ring)
    mate_up = send(up_sent, ds=half_ring)
    both = add_up([mine, after(from_core, gate_sent, up_sent)]).astype(BF16)
    both = y_sum(both)
    gate_part, up_part, both = lax.optimization_barrier((gate_part, up_part, both))

    half = jax.ShapeDtypeStruct((pair_tokens // NC, width), BF16)
    mine, other = run(
        functools.partial(third_kernel, update_factor, row_count),
        steps,
        [whole(product.shape)] * 4
        + [whole(part.shape), columns(token_count, chunk), columns(units, chunk)],
        [half, half],
        [columns(half.shape[0], chunk)] * 2,
        [pltpu.VMEM((pair_tokens, units), BF16), pltpu.VMEM((pair_tokens, token_count), BF16)],
        per_row * token_count * 3,
        "third",
        [gate_part, up_part, mate_gate, mate_up, hidden, cotangent, down_near],
    )
    pair = add_up([mine, send(other, dc=1)]).astype(BF16)
    both = cut(after(both, pair), NZ)
    both = add_up([both[0]] + [send(both[k], dz=k) for k in range(1, NZ)])
    forwarded = send(both[: slot_rows.shape[0]].astype(BF16), ds=1)
    dnormed = both[slot_rows.shape[0] :]
    first, second = cut(after(y_sum(pair), both), 2)
    own_parts = cut(jnp.where(first_half, first, second), NZ)
    mate_parts = cut(jnp.where(first_half, second, first), NZ)
    next_out = add_up(
        [next_values, own_parts[0]]
        + [send(mate_parts[k], ds=half_ring, dz=k) for k in range(NZ)]
        + [send(own_parts[k], dz=k) for k in range(1, NZ)]
    ).astype(BF16)
    scaled_grad = gain_row[None, :] * dnormed
    input_grad = (
        cotangent[:row_count].astype(F32)
        + row_scale * scaled_grad
        - values * row_scale**3 * jnp.mean(values * scaled_grad, axis=1, keepdims=True)
    ).astype(BF16)
    return (forwarded[None], input_grad[None], next_out[None])


def solution(mesh):
    in_specs = (
        P("section", "rep", None),
        P("section", "rep", None),
        P("section", "rep", None),
        P("section", None),
        P("section", None, "rep"),
        P("section", None, "rep"),
        P("section", "rep", None),
        P("section", None, None),
    )
    out_specs = (P("section", "rep", None), P("section", "rep", None), P("section", "rep", None))
    return jax.shard_map(
        per_device, mesh=mesh, in_specs=in_specs, out_specs=out_specs, check_vma=False
    )
```
